128 devices in a mesh: dp: 16 (over y, z), seq: 8 (over x, core).
Axes of the slice: x: 4, y: 4, z: 4, core: 2. Of those that a mesh axis runs over, the one named last changes fastest.
Arguments:
- tokens: bfloat16 [16384, 2880], P(('dp', 'seq')), may hold values from -6 to 6
- norm_gain: bfloat16 [2880], replicated, may hold values from 0.5 to 1.5
- router_weight: bfloat16 [2880, 64], replicated, may hold values from -0.109375 to 0.109375
- expert_ids: int32 [16384, 4], P(('dp', 'seq')), may hold values from 0 to 63, all different within a row; in each aligned block of 128 rows (0 to 127, 128 to 255, ...) at most 9 rows name the same one
- gate_up_words: int32 [128, 1440, 1440], P(('dp', 'seq')), may hold values from 0 to 255
- gate_up_scales: int32 [128, 90, 1440], P(('dp', 'seq')), may hold values from 119 to 121
- down_words: int32 [128, 720, 1440], P(('dp', 'seq')), may hold values from 0 to 255
- down_scales: int32 [128, 720, 90], P(('dp', 'seq')), may hold values from 119 to 121
- cotangent: bfloat16 [16384, 2880], P(('dp', 'seq')), may hold values from -6 to 6
Outputs:
- mixed: bfloat16 [16384, 2880], P(('dp', 'seq'))
- token_grad: bfloat16 [16384, 2880], P(('dp', 'seq'))
The draws below stay inside these ranges and needn't reach their ends.
Inputs may be any that keep to these rules, and one draw needn't show every extreme that they name: `expert_ids`: in each device's aligned block of 128 tokens no expert is named more than 9 times, a bound that some block reaches.
All inputs are finite; a program needn't handle non-finite values.
Results may differ from the reference program's by a relative error of at most 0.0029.
Values may be sent and summed in bfloat16 or wider, within the bound.
No kernel may reach another device: no remote copies, remote signals or barrier semaphores. Data moves between devices by JAX's collectives and lax.ppermute only.
A program may use at most 192 MiB of HBM per device.

```python
import math
import jax
import jax.numpy as jnp
import numpy as np
from jax import lax

D = 2880
HIDDEN_SIZE = 1440
TOP = 4
TOK_DEV = 128
HALF = 720
EXPERTS = 64
CAP = 9
TOKENS = 16384
N_DP = 16
N_SEQ = 8


def plant(entries, own_key, least, high):
    longest = entries.shape.index(max(entries.shape))
    spots = []
    for shift in (0, 1):
        where = [jax.random.randint(jax.random.fold_in(own_key, axis), (), 0, length) for axis, length in enumerate(entries.shape)]
        where[longest] = (where[longest] + shift) % entries.shape[longest]
        spots.append(tuple(where))
    return entries.at[spots[0]].set(least).at[spots[1]].set(high)


def levels(stream_key, extent, cuts, smallest, high):
    def one(position, blocks):
        steps = jax.random.uniform(jax.random.fold_in(jax.random.fold_in(stream_key, 6), position), (blocks,), jnp.float32, smallest / len(cuts), high / len(cuts))
        return jnp.repeat(jnp.exp(steps), extent[position] // blocks).reshape((-1,) + (1,) * (len(extent) - position - 1))

    level = one(*cuts[0])
    for cut in cuts[1:]:
        level = level * one(*cut)
    return level


def assign_block(stream_key, own, number, rows, count, top, reach, slope):
    sequence = jax.random.permutation(stream_key, count)
    packed, usual = shares(count, rows * top, reach, slope, True), shares(count, rows * top, reach, slope, False)
    places = jnp.arange(count)

    def named(tallies, turn):
        used = int((tallies > 0).sum())
        fixed = max(1, used // 4)
        shifted = fixed + (places - fixed + turn * (used - fixed)) % max(1, count - fixed)
        return jnp.zeros((count,), jnp.int32).at[sequence[jnp.where(places < fixed, places, shifted)]].set(jnp.asarray(tallies, jnp.int32))

    tallies = jnp.where(number % 4 == 0, named(packed, number // 4), named(usual, number - number // 4 - 1))
    mixed = jax.random.permutation(jax.random.fold_in(own, 3), count)
    giver, receiver = mixed[0:count // 2 * 2:2], mixed[1:count // 2 * 2:2]
    margin = jnp.minimum(tallies[giver] - 1, reach - tallies[receiver]) // 2
    margin = jnp.where((giver == sequence[0]) | (receiver == sequence[0]) | (tallies[receiver] == 0), 0, jnp.maximum(margin, 0))
    shifted = jax.random.randint(jax.random.fold_in(own, 4), (count // 2,), 0, 1 << 20) % (margin + 1)
    tallies = tallies.at[giver].add(-shifted).at[receiver].add(shifted)
    items = jnp.searchsorted(jnp.cumsum(tallies), jnp.arange(rows * top), side="right").astype(jnp.int32)
    listing = items.reshape(top, rows).T
    listing = listing[jax.random.permutation(jax.random.fold_in(own, 1), rows)]
    turn = jax.random.randint(jax.random.fold_in(own, 2), (rows, 1), 0, top)
    return jnp.take_along_axis(listing, (jnp.arange(top)[None, :] + turn) % top, axis=1)


def shares(amount, total, most, lean, full):
    loads = [(1 << 20) // math.isqrt(grade ** lean) + 1 for grade in range(1, amount + 1)]
    largest = most if full else min(most, max(-(-total // amount), total * loads[0] // sum(loads)))
    least = 1 if total - largest >= amount - 1 else 0
    counts, rest = [largest] + [least] * (amount - 1), total - largest - least * (amount - 1)
    while rest > 0:
        candidates = [i for i in range(1, amount) if counts[i] < largest] or [i for i in range(1, amount) if counts[i] < most]
        whole, remaining = sum([loads[i] for i in candidates]), rest
        for i in candidates:
            addition = min(most - counts[i], max(1, remaining * loads[i] // whole), rest)
            counts[i] = counts[i] + addition
            rest = rest - addition
    return np.array(counts)


def normal_values(stream_key, extent, width, bound, pieces=(), kind=jnp.bfloat16):
    result = width * jax.random.normal(stream_key, extent, jnp.float32)
    if pieces:
        result = result * levels(stream_key, extent, pieces, -0.22, 0.18)
    return jnp.clip(result, -bound, bound).astype(kind)


def setup_inputs(seed: int = 0) -> dict:
    keys = jax.random.split(jax.random.key(seed), 10)
    tokens = normal_values(keys[0], (TOKENS, D), 1.0, 6.0, ((0, 128),))
    norm_gain = jnp.clip(1.0 + 0.1 * jax.random.normal(keys[1], (D,), jnp.float32), 0.5, 1.5).astype(jnp.bfloat16)
    router_weight = normal_values(keys[2], (D, EXPERTS), D ** -0.5, 0.109375)
    expert_ids_keys = jax.random.split(jax.random.fold_in(keys[3], 1), TOKENS // TOK_DEV)
    expert_ids_turns = jax.random.permutation(jax.random.fold_in(keys[3], 3), TOKENS // TOK_DEV)
    expert_ids = jax.vmap(lambda own, number: assign_block(jax.random.fold_in(keys[3], 2), own, number, TOK_DEV, EXPERTS, TOP, CAP, 2))(expert_ids_keys, expert_ids_turns).reshape((TOKENS, TOP))
    gate_up_words = plant(jax.random.randint(keys[4], (2 * EXPERTS, D // 2, HIDDEN_SIZE), 0, 256), jax.random.fold_in(keys[4], 1), 0, 255).astype(jnp.int32)
    gate_up_scales = plant(jax.random.randint(keys[5], (2 * EXPERTS, D // 32, HIDDEN_SIZE), 119, 122), jax.random.fold_in(keys[5], 1), 119, 121).astype(jnp.int32)
    down_words = plant(jax.random.randint(keys[6], (2 * EXPERTS, HALF, D // 2), 0, 256), jax.random.fold_in(keys[6], 1), 0, 255).astype(jnp.int32)
    down_scales = plant(jax.random.randint(keys[7], (2 * EXPERTS, HALF, D // 32), 119, 122), jax.random.fold_in(keys[7], 1), 119, 121).astype(jnp.int32)
    cotangent = normal_values(keys[8], (TOKENS, D), 1.0, 6.0, ((0, 128),))
    return dict(tokens=tokens, norm_gain=norm_gain, router_weight=router_weight, expert_ids=expert_ids, gate_up_words=gate_up_words, gate_up_scales=gate_up_scales, down_words=down_words, down_scales=down_scales, cotangent=cotangent)


glu_slope = 1.702
norm_epsilon = 1e-05

def small_float(code_values):
    sign_part = code_values // 8
    level_code = code_values % 8
    exponent = level_code // 2
    mantissa = (level_code % 2).astype(jnp.float32)
    scaled = jnp.exp2((exponent - 1).astype(jnp.float32)) * (1.0 + 0.5 * mantissa)
    magnitude = jnp.where(exponent == 0, 0.5 * mantissa, scaled)
    return jnp.where(sign_part == 1, -magnitude, magnitude)

def unpack_rows(code_words, scale_codes):
    groups = scale_codes.shape[0]
    columns = code_words.shape[1]
    factor = jnp.exp2((scale_codes - 127).astype(jnp.float32))[:, None, :]
    shaped = code_words.reshape(groups, -1, columns)
    low_vals = (small_float(shaped % 16) * factor).astype(jnp.bfloat16)
    high_vals = (small_float(shaped // 16) * factor).astype(jnp.bfloat16)
    return jnp.stack([low_vals, high_vals], axis=2).reshape(-1, columns)

def unpack_cols(code_words, scale_codes):
    lines = code_words.shape[0]
    groups = scale_codes.shape[1]
    factor = jnp.exp2((scale_codes - 127).astype(jnp.float32))[:, :, None]
    shaped = code_words.reshape(lines, groups, -1)
    low_vals = (small_float(shaped % 16) * factor).astype(jnp.bfloat16)
    high_vals = (small_float(shaped // 16) * factor).astype(jnp.bfloat16)
    return jnp.stack([low_vals, high_vals], axis=3).reshape(lines, -1)

def expert_half(rows_in, grads_in, gate_up, down_proj):
    half_units = down_proj.shape[0]
    pre_act = jnp.dot(rows_in, gate_up, preferred_element_type=jnp.float32)
    gate_pre = pre_act[:, :half_units]
    up_pre = pre_act[:, half_units:]
    sig_gate = jax.nn.sigmoid(glu_slope * gate_pre)
    glu_gate = gate_pre * sig_gate
    active = (glu_gate * (up_pre + 1.0)).astype(jnp.bfloat16)
    part_out = jnp.dot(active, down_proj, preferred_element_type=jnp.float32).astype(jnp.bfloat16)
    back_act = lax.dot_general(grads_in, down_proj, (((1,), (1,)), ((), ())), preferred_element_type=jnp.float32)
    slope_term = sig_gate + glu_slope * glu_gate * (1.0 - sig_gate)
    grad_pre = jnp.concatenate([back_act * (up_pre + 1.0) * slope_term, back_act * glu_gate], axis=1).astype(jnp.bfloat16)
    part_back = lax.dot_general(grad_pre, gate_up, (((1,), (1,)), ((), ())), preferred_element_type=jnp.float32).astype(jnp.bfloat16)
    return (part_out, part_back)

def reference(tokens, norm_gain, router_weight, expert_ids, gate_up_words, gate_up_scales, down_words, down_scales, cotangent):
    device_total = N_DP * N_SEQ
    tok_f = tokens.astype(jnp.float32)
    cot_f = cotangent.astype(jnp.float32)
    gain_f = norm_gain.astype(jnp.float32)
    inv_rms = lax.rsqrt(lax.optimization_barrier(jnp.mean(tok_f * tok_f, axis=1, keepdims=True)) + norm_epsilon)
    normed = (tok_f * inv_rms * gain_f).astype(jnp.bfloat16)
    logits = jnp.dot(normed, router_weight, preferred_element_type=jnp.float32)
    one_hot = expert_ids[:, :, None] == jnp.arange(EXPERTS, dtype=jnp.int32)
    picked = lax.optimization_barrier(jnp.sum(jnp.where(one_hot, logits[:, None, :], 0.0), axis=2))
    raised = jnp.exp(picked)
    probs = raised / lax.optimization_barrier(jnp.sum(raised, axis=1, keepdims=True))
    flat_probs = probs.reshape(-1)
    pair_count = TOKENS * TOP
    flat_hot = one_hot.reshape(device_total, TOK_DEV * TOP, EXPERTS).astype(jnp.int32)
    running = jnp.cumsum(flat_hot, axis=1)
    slot_of = (lax.optimization_barrier(jnp.sum(running * flat_hot, axis=2)) - 1).reshape(-1).astype(jnp.int32)
    pair_index = jnp.arange(pair_count, dtype=jnp.int32)
    device_of = pair_index // (TOK_DEV * TOP)
    flat_ids = expert_ids.reshape(-1).astype(jnp.int32)
    table = jnp.full((EXPERTS, device_total * CAP), pair_count, jnp.int32)
    table = table.at[flat_ids, device_of * CAP + slot_of].set(pair_index)

    def per_expert(carried, expert):
        mixed_acc, back_acc, dprob_acc = carried
        slot_pairs = table[expert]
        filled = slot_pairs < pair_count
        safe_pair = jnp.minimum(slot_pairs, pair_count - 1)
        safe_token = safe_pair // TOP
        rows_in = jnp.where(filled[:, None], normed[safe_token], 0)
        grads_in = jnp.where(filled[:, None], (flat_probs[safe_pair][:, None] * cot_f[safe_token]).astype(jnp.bfloat16), 0)
        total_out = jnp.zeros((slot_pairs.shape[0], D), jnp.float32)
        total_back = jnp.zeros((slot_pairs.shape[0], D), jnp.float32)
        for half_index in range(2):
            which = 2 * expert + half_index
            gate_up = unpack_rows(lax.dynamic_index_in_dim(gate_up_words, which, 0, keepdims=False), lax.dynamic_index_in_dim(gate_up_scales, which, 0, keepdims=False))
            down_proj = unpack_cols(lax.dynamic_index_in_dim(down_words, which, 0, keepdims=False), lax.dynamic_index_in_dim(down_scales, which, 0, keepdims=False))
            part_out, part_back = expert_half(rows_in, grads_in, gate_up, down_proj)
            total_out = total_out + part_out.astype(jnp.float32)
            total_back = total_back + part_back.astype(jnp.float32)
        weight = jnp.where(filled, flat_probs[safe_pair], 0.0)
        mixed_acc = mixed_acc.at[safe_token].add(weight[:, None] * total_out)
        back_acc = back_acc.at[safe_token].add(jnp.where(filled[:, None], total_back, 0.0))
        dprob_acc = dprob_acc.at[safe_pair].add(jnp.where(filled, lax.optimization_barrier(jnp.sum(cot_f[safe_token] * total_out, axis=1)), 0.0))
        return ((mixed_acc, back_acc, dprob_acc), None)
    start = (jnp.zeros((TOKENS, D), jnp.float32), jnp.zeros((TOKENS, D), jnp.float32), jnp.zeros((pair_count,), jnp.float32))
    (mixed_acc, back_acc, dprob_acc), _ = lax.scan(per_expert, start, jnp.arange(EXPERTS, dtype=jnp.int32))
    mixed = (tok_f + mixed_acc).astype(jnp.bfloat16)
    dprob = dprob_acc.reshape(TOKENS, TOP)
    dpicked = probs * (dprob - lax.optimization_barrier(jnp.sum(probs * dprob, axis=1, keepdims=True)))
    dlogits = lax.optimization_barrier(jnp.sum(jnp.where(one_hot, dpicked[:, :, None], 0.0), axis=1))
    dnormed = jnp.dot(dlogits, router_weight.astype(jnp.float32).T, precision=lax.Precision.HIGHEST) + back_acc
    gain_grad = gain_f * dnormed
    token_grad = cot_f + inv_rms * gain_grad - tok_f * (inv_rms * inv_rms * inv_rms) * lax.optimization_barrier(jnp.mean(gain_grad * tok_f, axis=1, keepdims=True))
    return (mixed, token_grad.astype(jnp.bfloat16))
```

```python
import functools

import jax
import jax.numpy as jnp
from jax import lax
from jax.experimental import pallas as pl
from jax.experimental.pallas import tpu as pltpu
from jax.sharding import Mesh, PartitionSpec as P

glu_slope = 1.702
norm_epsilon = 1e-05

LANE = 128
PAIR = 2 * LANE
SLOTS = 8
F32 = jnp.float32
BF16 = jnp.bfloat16


def up_to(n, m):
    return -(-n // m) * m


def mm(a, b):
    return jnp.dot(a, b, preferred_element_type=F32)


def mm_nt(a, b):
    return lax.dot_general(a, b, (((1,), (1,)), ((), ())), preferred_element_type=F32)


def iota(shape, dim):
    return lax.broadcasted_iota(jnp.int32, shape, dim)


def mm_tn(a, b):
    return lax.dot_general(a, b, (((0,), (0,)), ((), ())), preferred_element_type=F32)


def split_matrix(n):
    nat, col = iota((n, n), 0), iota((n, n), 1)
    half = n // 2
    src = jnp.where(col < half, 2 * col, 2 * (col - half) + 1)
    return (nat == src).astype(F32).astype(BF16)


def feature_blocks(width):
    full = width // PAIR * PAIR
    blocks = [(start, PAIR, split_matrix(PAIR)) for start in range(0, full, PAIR)]
    return blocks + ([(full, width - full, split_matrix(width - full))] if width > full else [])


def order_columns(src_ref, dst_ref):
    for start, size, hot in feature_blocks(src_ref.shape[1]):
        dst_ref[:, start : start + size] = mm(src_ref[:, start : start + size], hot).astype(BF16)


def order_rows(src_ref, dst_ref):
    for start, size, hot in feature_blocks(src_ref.shape[0]):
        dst_ref[:, start : start + size] = mm_tn(src_ref[start : start + size, :], hot).astype(BF16)


def restore_rows(load, dst_ref):
    for start, size, hot in feature_blocks(dst_ref.shape[0]):
        dst_ref[start : start + size, :] = mm_nt(hot, load(start, size)).astype(BF16)


def tail_geometry(width):
    tail_at = up_to(width, LANE)
    tail = up_to(-(-tail_at // SLOTS), LANE)
    return tail_at, tail


def slot_hot(slot_t):
    experts, toks = slot_t.shape
    s_idx = iota((experts, SLOTS, toks), 1).astype(F32)
    hot = (slot_t[:, None, :] == s_idx).astype(F32)
    return hot.reshape(experts * SLOTS, toks), (slot_t == float(SLOTS)).astype(F32)


def put_tail(msg_ref, nine, nine_sc, fold_sc, tail_at, tail, width):
    experts = nine.shape[0]
    nine_sc[:, width:] = jnp.zeros((experts, nine_sc.shape[1] - width), F32)
    nine_sc[:, :width] = nine
    fold_lanes(msg_ref, nine_sc, fold_sc, experts, tail_at, tail)


def fold_lanes(msg_ref, nine, fold_sc, experts, tail_at, tail):
    for j in range(tail // LANE):
        for r in range(SLOTS):
            at = r * tail + j * LANE
            fold_sc[j, pl.ds(r, experts, stride=SLOTS), :] = nine[:, at : at + LANE]
        at = tail_at + j * LANE
        msg_ref[:, at : at + LANE] = fold_sc[j].astype(BF16)


def get_tail(msg_ref, fold_sc, put, tail_at, tail, experts):
    for j in range(tail // LANE):
        at = tail_at + j * LANE
        fold_sc[j] = msg_ref[:, at : at + LANE].astype(F32)
        for r in range(SLOTS):
            put(r * tail + j * LANE, fold_sc[j, pl.ds(r, experts, stride=SLOTS), :].astype(BF16))


def dispatch_rows_kernel(
    tok_ref, gain_ref, router_ref, ids_ref,
    msg_ref, prob_ref, slot_ref, tokp_ref, gainp_ref, routerp_ref,
    normp_sc, gain_sc, nine_sc, fold_sc,
):
    width, toks = tok_ref.shape
    top = ids_ref.shape[0]
    experts = router_ref.shape[0]
    tail_at, tail = tail_geometry(width)
    order_rows(tok_ref, tokp_ref)
    gain_sc[...] = jnp.broadcast_to(gain_ref[...], gain_sc.shape)
    order_columns(gain_sc, gainp_ref)
    order_columns(router_ref, routerp_ref)
    tok = tokp_ref[...].astype(F32)
    inv = lax.rsqrt(jnp.sum(tok * tok, axis=1, keepdims=True) / width + norm_epsilon)
    normp_sc[...] = (tok * inv * gainp_ref[0:1, :].astype(F32)).astype(BF16)
    logits = mm_nt(routerp_ref[...], normp_sc[...])
    e_idx = iota((experts, toks), 0)
    chosen = e_idx == ids_ref[0:1, :]
    for k in range(1, top):
        chosen = chosen | (e_idx == ids_ref[k : k + 1, :])
    raised = jnp.where(chosen, jnp.exp(logits), 0.0)
    prob_ref[...] = raised / jnp.sum(raised, axis=0, keepdims=True)
    earlier = (iota((toks, toks), 0) < iota((toks, toks), 1)).astype(F32).astype(BF16)
    rank = mm(chosen.astype(F32).astype(BF16), earlier)
    slot = jnp.where(chosen, rank, -1.0)
    slot_ref[...] = slot
    hot, hot_nine = slot_hot(slot)
    hot = hot.astype(BF16)
    for start in range(0, width, 2 * PAIR):
        stop = min(start + 2 * PAIR, width)
        msg_ref[:, start:stop] = mm(hot, normp_sc[:, start:stop]).astype(BF16)
    msg_ref[:, width:tail_at] = jnp.zeros((msg_ref.shape[0], tail_at - width), BF16)
    nine = mm(hot_nine.astype(BF16), normp_sc[...])
    put_tail(msg_ref, nine, nine_sc, fold_sc, tail_at, tail, width)


def dispatch_grads_kernel(
    cot_ref, prob_ref, slot_ref,
    msg_ref, cotp_ref,
    nine_sc, fold_sc,
):
    width, toks = cot_ref.shape
    experts = prob_ref.shape[0]
    tail_at, tail = tail_geometry(width)
    order_rows(cot_ref, cotp_ref)
    prob = prob_ref[...]
    hot, hot_nine = slot_hot(slot_ref[...])
    spread = jnp.broadcast_to(prob[:, None, :], (experts, SLOTS, toks)).reshape(experts * SLOTS, toks)
    row_prob = jnp.sum(hot * spread, axis=1, keepdims=True)
    nine_prob = jnp.sum(hot_nine * prob, axis=1, keepdims=True)
    hot = hot.astype(BF16)
    for start in range(0, width, 2 * PAIR):
        stop = min(start + 2 * PAIR, width)
        msg_ref[:, start:stop] = (mm(hot, cotp_ref[:, start:stop]) * row_prob).astype(BF16)
    msg_ref[:, width:tail_at] = jnp.zeros((msg_ref.shape[0], tail_at - width), BF16)
    nine = mm(hot_nine.astype(BF16), cotp_ref[...]) * nine_prob
    put_tail(msg_ref, nine, nine_sc, fold_sc, tail_at, tail, width)


def code_value(code):
    m = code & 7
    mag = jnp.maximum(jnp.maximum(m, 2 * m - 4), 4 * m - 16)
    return jnp.where((code & 8) != 0, -mag, mag).astype(F32)


def decode_rows_kernel(rest, words_ref, scales_ref, out_ref, factor_sc):
    groups = scales_ref.shape[0]
    columns = words_ref.shape[1]
    out_ref[:, columns:] = jnp.zeros((out_ref.shape[0], out_ref.shape[1] - columns), BF16)
    per = words_ref.shape[0] // groups
    step = pl.program_id(0)
    last = pl.num_programs(0) - 1
    factor_sc[...] = jnp.exp2((scales_ref[...] - 128).astype(F32))

    def group(g, low_at, high_at):
        for start in range(0, columns, 4 * LANE):
            stop = min(start + 4 * LANE, columns)
            w = words_ref[g * per : (g + 1) * per, start:stop]
            f = factor_sc[g : g + 1, start:stop]
            out_ref[low_at : low_at + per, start:stop] = (code_value(w) * f).astype(BF16)
            out_ref[high_at : high_at + per, start:stop] = (code_value(w >> 4) * f).astype(BF16)

    @pl.when(step < last)
    def _():
        for g in range(groups):
            group(g, g * per, LANE + g * per)

    @pl.when(step == last)
    def _():
        for g in range(rest // per):
            group(g, g * per, rest + g * per)


def decode_cols_kernel(words_ref, scales_ref, out_ref, factor_sc):
    rows, columns = words_ref.shape
    groups = scales_ref.shape[1]
    per = columns // groups
    step_rows = 16
    expand = (iota((groups, columns), 0) == iota((groups, columns), 1) // per).astype(F32).astype(BF16)
    factor_sc[...] = mm(jnp.exp2((scales_ref[...] - 128).astype(F32)).astype(BF16), expand)
    full = columns // LANE * LANE
    rest = columns - full

    def body(i, carry):
        r = pl.ds(pl.multiple_of(i * step_rows, step_rows), step_rows)
        for start in range(0, full, LANE):
            w = words_ref[r, start : start + LANE]
            f = factor_sc[r, start : start + LANE]
            out_ref[r, 2 * start : 2 * start + LANE] = (code_value(w) * f).astype(BF16)
            out_ref[r, 2 * start + LANE : 2 * start + PAIR] = (code_value(w >> 4) * f).astype(BF16)
        if rest:
            w = words_ref[r, full:columns]
            f = factor_sc[r, full:columns]
            both = jnp.concatenate([code_value(w) * f, code_value(w >> 4) * f], axis=1)
            out_ref[r, 2 * full :] = both.astype(BF16)
        return carry

    lax.fori_loop(0, rows // step_rows, body, 0)


def rounded(half_sum):
    return half_sum.astype(BF16).astype(F32)


def ffn_forward_kernel(
    x_ref, gu_own_ref, gu_oth_ref, down_own_ref, down_oth_ref,
    out_ref, coef_own_ref, coef_oth_ref,
    x_sc, pre_sc, act_own_sc, act_oth_sc, res_sc, fold_sc,
    *, width, half, n_up, n_down,
):
    step = pl.program_id(0)
    rows = x_ref.shape[0]
    experts = rows // SLOTS
    all_rows = rows + experts
    tail_at, tail = tail_geometry(width)
    tile_up = gu_own_ref.shape[1]
    tile_down = down_own_ref.shape[1]
    padded = pre_sc.shape[1]

    @pl.when(step == 0)
    def _():
        x_sc[:rows, :width] = x_ref[:, :width]

        def put(at, value):
            x_sc[rows:, at : at + LANE] = value

        get_tail(x_ref, fold_sc, put, tail_at, tail, experts)

    def up(gu_ref, index):
        at = pl.multiple_of(index * tile_up, tile_up)
        pre_sc[:, pl.ds(at, tile_up)] = mm(x_sc[:, :width], gu_ref[...])

    def finish(act_sc, coef_ref):
        chunk = 16

        def body(i, carry):
            r = pl.ds(pl.multiple_of(i * chunk, chunk), chunk)
            pre = pre_sc[r, :]
            wide = act_sc.shape[1]
            gate = pre[:, :wide]
            lift = pltpu.roll(pre, padded - half, 1)[:, :wide] + 1.0
            sig = jax.nn.sigmoid(glu_slope * gate)
            glu = gate * sig
            act_sc[r, :] = (glu * lift).astype(BF16)
            slope = sig + glu_slope * glu * (1.0 - sig)
            grad_gate = lift * slope
            zero = jnp.zeros((chunk, padded - wide), F32)
            grad_up = pltpu.roll(jnp.concatenate([glu, zero], axis=1), half, 1)
            lanes = iota((chunk, padded), 1)
            coef_ref[r, :] = jnp.where(
                lanes < half, jnp.concatenate([grad_gate, zero], axis=1), grad_up
            )
            return carry

        lax.fori_loop(0, all_rows // chunk, body, 0)

    @pl.when(step < n_up)
    def _():
        up(gu_own_ref, step)

    @pl.when(step == n_up - 1)
    def _():
        finish(act_own_sc, coef_own_ref)

    @pl.when((step >= n_up) & (step < 2 * n_up))
    def _():
        up(gu_oth_ref, step - n_up)

    @pl.when(step == 2 * n_up - 1)
    def _():
        finish(act_oth_sc, coef_oth_ref)

    @pl.when(step >= 2 * n_up)
    def _():
        at = pl.multiple_of((step - 2 * n_up) * tile_down, tile_down)
        res_sc[:, pl.ds(at, tile_down)] = rounded(
            mm(act_own_sc[:, :half], down_own_ref[...])
        ) + rounded(mm(act_oth_sc[:, :half], down_oth_ref[...]))

    @pl.when(step == 2 * n_up + n_down - 1)
    def _():
        emit(out_ref, res_sc, fold_sc, rows, experts, tail_at, tail)


def emit(out_ref, res_sc, fold_sc, rows, experts, tail_at, tail):
    chunk = 32

    def body(i, carry):
        r = pl.ds(pl.multiple_of(i * chunk, chunk), chunk)
        out_ref[r, :tail_at] = res_sc[r, :tail_at].astype(BF16)
        return carry

    lax.fori_loop(0, rows // chunk, body, 0)
    fold_lanes(out_ref, res_sc.at[rows:, :], fold_sc, experts, tail_at, tail)


def ffn_backward_kernel(
    g_ref, coef_own_ref, coef_oth_ref, down_own_ref, down_oth_ref, gu_own_ref, gu_oth_ref,
    out_ref,
    g_sc, back_sc, pre_own_sc, pre_oth_sc, res_sc, fold_sc,
    *, width, half, inner, n_back,
):
    step = pl.program_id(0)
    rows = g_ref.shape[0]
    experts = rows // SLOTS
    all_rows = rows + experts
    tail_at, tail = tail_geometry(width)
    tile = gu_own_ref.shape[0]
    padded = coef_own_ref.shape[1]

    @pl.when(step == 0)
    def _():
        g_sc[:rows, :width] = g_ref[:, :width]

        def put(at, value):
            g_sc[rows:, at : at + LANE] = value

        get_tail(g_ref, fold_sc, put, tail_at, tail, experts)

    def finish(coef_ref, pre_sc):
        chunk = 16

        def body(i, carry):
            r = pl.ds(pl.multiple_of(i * chunk, chunk), chunk)
            back = back_sc[r, :]
            lanes = iota((chunk, padded), 1)
            twice = jnp.where(lanes < half, back, pltpu.roll(back, half, 1))
            pre_sc[r, :] = (twice * coef_ref[r, :]).astype(BF16)
            return carry

        lax.fori_loop(0, all_rows // chunk, body, 0)

    @pl.when(step == 0)
    def _():
        back_sc[:, :half] = mm_nt(g_sc[:, :width], down_own_ref[...])
        finish(coef_own_ref, pre_own_sc)

    @pl.when(step == 1)
    def _():
        back_sc[:, :half] = mm_nt(g_sc[:, :width], down_oth_ref[...])
        finish(coef_oth_ref, pre_oth_sc)

    @pl.when(step >= 2)
    def _():
        at = pl.multiple_of((step - 2) * tile, tile)
        res_sc[:, pl.ds(at, tile)] = rounded(
            mm_nt(pre_own_sc[:, :inner], gu_own_ref[:, :inner])
        ) + rounded(mm_nt(pre_oth_sc[:, :inner], gu_oth_ref[:, :inner]))

    @pl.when(step == 2 + n_back - 1)
    def _():
        emit(out_ref, res_sc, fold_sc, rows, experts, tail_at, tail)


def combine_out_kernel(
    msg_ref, tokp_ref, cotp_ref, prob_ref, slot_ref, router_ref,
    mixed_ref, dnormed_ref,
    nine_sc, fold_sc, mix_sc,
):
    toks, width = tokp_ref.shape
    experts = prob_ref.shape[0]
    tail_at, tail = tail_geometry(width)

    def put(at, value):
        nine_sc[:, at : at + LANE] = value

    get_tail(msg_ref, fold_sc, put, tail_at, tail, experts)
    prob = prob_ref[...]
    hot, hot_nine = slot_hot(slot_ref[...])
    spread = jnp.broadcast_to(prob[:, None, :], (experts, SLOTS, toks)).reshape(experts * SLOTS, toks)
    weight = jnp.concatenate([hot * spread, hot_nine * prob], axis=0).T
    high = weight.astype(BF16)
    low = (weight - high.astype(F32)).astype(BF16)
    main = experts * SLOTS
    for start in range(0, width, 2 * PAIR):
        stop = min(start + 2 * PAIR, width)
        rows = msg_ref[:, start:stop]
        nine = nine_sc[:, start:stop]
        total = tokp_ref[:, start:stop].astype(F32)
        total = total + mm(high[:, :main], rows) + mm(low[:, :main], rows)
        total = total + mm(high[:, main:], nine) + mm(low[:, main:], nine)
        mix_sc[:, start:stop] = total.astype(BF16)

    restore_rows(lambda start, size: mix_sc[:, start : start + size], mixed_ref)
    cot = cotp_ref[...]
    along = (mm_nt(msg_ref[:, :width], cot) * hot).reshape(experts, SLOTS, toks)
    dprob = jnp.sum(along, axis=1) + mm_nt(nine_sc[:, :width], cot) * hot_nine
    dlogits_t = prob * (dprob - jnp.sum(prob * dprob, axis=0, keepdims=True))
    dlogits = dlogits_t.T
    first = dlogits.astype(BF16)
    left = dlogits - first.astype(F32)
    second = left.astype(BF16)
    third = (left - second.astype(F32)).astype(BF16)
    router = router_ref[...]
    dnormed_ref[...] = mm(first, router) + mm(second, router) + mm(third, router)


def combine_back_kernel(
    msg_ref, tokp_ref, cotp_ref, slot_ref, gain_ref, dnormed_ref,
    grad_ref,
    nine_sc, fold_sc, sum_sc,
):
    toks, width = tokp_ref.shape
    experts = slot_ref.shape[0]
    tail_at, tail = tail_geometry(width)

    def put(at, value):
        nine_sc[:, at : at + LANE] = value

    get_tail(msg_ref, fold_sc, put, tail_at, tail, experts)
    hot, hot_nine = slot_hot(slot_ref[...])
    pick = jnp.concatenate([hot, hot_nine], axis=0).T.astype(BF16)
    main = experts * SLOTS
    tok = tokp_ref[...].astype(F32)
    inv = lax.rsqrt(jnp.sum(tok * tok, axis=1, keepdims=True) / width + norm_epsilon)
    along = jnp.zeros((toks, 1), F32)
    for start in range(0, width, 2 * PAIR):
        stop = min(start + 2 * PAIR, width)
        total = mm(pick[:, :main], msg_ref[:, start:stop]) + mm(pick[:, main:], nine_sc[:, start:stop])
        total = (total + dnormed_ref[:, start:stop]) * gain_ref[0:1, start:stop].astype(F32)
        sum_sc[:, start:stop] = total
        along = along + jnp.sum(total * tokp_ref[:, start:stop].astype(F32), axis=1, keepdims=True)
    cube = inv * inv * inv * (along / width)

    def load(start, size):
        value = (
            cotp_ref[:, start : start + size].astype(F32)
            + inv * sum_sc[:, start : start + size]
            - tokp_ref[:, start : start + size].astype(F32) * cube
        )
        return value.astype(BF16)

    restore_rows(load, grad_ref)


def params(mib):
    return pltpu.CompilerParams(vmem_limit_bytes=mib * 1024 * 1024)


def once(shape):
    return pl.BlockSpec(shape, lambda *_: (0,) * len(shape), pipeline_mode=pl.Buffered(1))


def simple_call(kernel, outs, scratch):
    return pl.pallas_call(
        kernel, out_shape=outs, scratch_shapes=scratch, compiler_params=params(24)
    )


def struct(shape, dtype):
    return jax.ShapeDtypeStruct(shape, dtype)


def shards(
    tokens, norm_gain, router_weight, expert_ids,
    gate_up_words, gate_up_scales, down_words, down_scales, cotangent,
):
    toks, width = tokens.shape
    experts = router_weight.shape[1]
    word_rows, inner = gate_up_words.shape[1:]
    half, word_cols = down_words.shape[1:]
    tail_at, tail = tail_geometry(width)
    msg_width = tail_at + tail
    rows = experts * SLOTS
    all_rows = rows + experts
    wide = SLOTS * tail
    padded = up_to(inner, PAIR)
    gain = norm_gain.reshape(1, width)

    nine_f = pltpu.VMEM((experts, wide), F32)
    nine_b = pltpu.VMEM((experts, wide), BF16)
    fold = pltpu.VMEM((tail // LANE, rows, LANE), F32)
    msg = struct((rows, msg_width), BF16)

    table = struct((experts, toks), F32)
    block = struct((toks, width), BF16)
    row_msg, prob, slot, tokp, gainp, routerp = simple_call(
        dispatch_rows_kernel,
        (msg, table, table, block, struct((16, width), BF16), struct((experts, width), BF16)),
        [pltpu.VMEM((toks, width), BF16), pltpu.VMEM((16, width), BF16), nine_f, fold],
    )(tokens.T, gain, router_weight.T, expert_ids.T)
    row_msg, gate_up_words, down_words = lax.optimization_barrier(
        (row_msg, gate_up_words, down_words)
    )

    def exchange(message):
        shaped = message.reshape(experts, SLOTS, msg_width)
        swapped = lax.all_to_all(shaped, ("dp", "x"), 0, 0, tiled=True)
        return swapped.reshape(rows, msg_width)

    rows_in = exchange(row_msg)
    grad_msg, cotp = simple_call(
        dispatch_grads_kernel, (msg, block), [nine_f, fold]
    )(cotangent.T, prob, slot)
    grads_in = exchange(grad_msg)

    group_rows = word_rows // gate_up_scales.shape[1]
    steps = -(-word_rows // LANE)
    gate_up = pl.pallas_call(
        functools.partial(decode_rows_kernel, word_rows - (steps - 1) * LANE),
        out_shape=struct((2 * word_rows, padded), BF16),
        grid=(steps,),
        in_specs=[
            pl.BlockSpec((LANE, inner), lambda i: (i, 0)),
            pl.BlockSpec((LANE // group_rows, inner), lambda i: (i, 0)),
        ],
        out_specs=pl.BlockSpec((PAIR, padded), lambda i: (i, 0)),
        scratch_shapes=[pltpu.VMEM((LANE // group_rows, inner), F32)],
        compiler_params=params(24),
        name="decode_gate_up",
    )(gate_up_words[0], gate_up_scales[0])
    down_rows = 144
    down = pl.pallas_call(
        decode_cols_kernel,
        out_shape=struct((half, 2 * word_cols), BF16),
        grid=(half // down_rows,),
        in_specs=[
            pl.BlockSpec((down_rows, word_cols), lambda i: (i, 0)),
            pl.BlockSpec((down_rows, down_scales.shape[2]), lambda i: (i, 0)),
        ],
        out_specs=pl.BlockSpec((down_rows, 2 * word_cols), lambda i: (i, 0)),
        scratch_shapes=[pltpu.VMEM((down_rows, word_cols), F32)],
        compiler_params=params(24),
        name="decode_down",
    )(down_words[0], down_scales[0])
    swap = [(0, 1), (1, 0)]
    gate_up_other = lax.ppermute(gate_up, "core", swap)
    down_other = lax.ppermute(down, "core", swap)

    tile = 512
    n_up = -(-inner // tile)
    n_down = -(-width // tile)
    half_wide = up_to(half, LANE)
    coef = struct((all_rows, padded), F32)

    def clip(i, low, count):
        return jnp.clip(i - low, 0, count - 1)

    out_msg, coef_own, coef_oth = pl.pallas_call(
        functools.partial(ffn_forward_kernel, width=width, half=half, n_up=n_up, n_down=n_down),
        out_shape=(msg, coef, coef),
        grid=(2 * n_up + n_down,),
        in_specs=[
            once((rows, msg_width)),
            pl.BlockSpec((width, tile), lambda i: (0, clip(i, 0, n_up))),
            pl.BlockSpec((width, tile), lambda i: (0, clip(i, n_up, n_up))),
            pl.BlockSpec((half, tile), lambda i: (0, clip(i, 2 * n_up, n_down))),
            pl.BlockSpec((half, tile), lambda i: (0, clip(i, 2 * n_up, n_down))),
        ],
        out_specs=(once((rows, msg_width)), once((all_rows, padded)), once((all_rows, padded))),
        scratch_shapes=[
            pltpu.VMEM((all_rows, wide), BF16),
            pltpu.VMEM((all_rows, padded), F32),
            pltpu.VMEM((all_rows, half_wide), BF16),
            pltpu.VMEM((all_rows, half_wide), BF16),
            pltpu.VMEM((all_rows, n_down * tile), F32),
            fold,
        ],
        compiler_params=params(52),
        name="ffn_forward",
    )(rows_in, gate_up, gate_up_other, down, down_other)
    outs_in = exchange(out_msg)

    back_msg = pl.pallas_call(
        functools.partial(
            ffn_backward_kernel, width=width, half=half, inner=inner, n_back=n_down
        ),
        out_shape=msg,
        grid=(2 + n_down,),
        in_specs=[
            once((rows, msg_width)),
            once((all_rows, padded)),
            once((all_rows, padded)),
            once((half, width)),
            once((half, width)),
            pl.BlockSpec((tile, padded), lambda i: (clip(i, 2, n_down), 0)),
            pl.BlockSpec((tile, padded), lambda i: (clip(i, 2, n_down), 0)),
        ],
        out_specs=once((rows, msg_width)),
        scratch_shapes=[
            pltpu.VMEM((all_rows, wide), BF16),
            pltpu.VMEM((all_rows, padded), F32),
            pltpu.VMEM((all_rows, padded), BF16),
            pltpu.VMEM((all_rows, padded), BF16),
            pltpu.VMEM((all_rows, n_down * tile), F32),
            fold,
        ],
        compiler_params=params(52),
        name="ffn_backward",
    )(grads_in, coef_own, coef_oth, down, down_other, gate_up, gate_up_other)
    backs_in = exchange(back_msg)

    turned = struct((width, toks), BF16)
    mixed, dnormed = simple_call(
        combine_out_kernel,
        (turned, struct((toks, width), F32)),
        [nine_b, fold, pltpu.VMEM((toks, width), BF16)],
    )(outs_in, tokp, cotp, prob, slot, routerp)
    token_grad = simple_call(
        combine_back_kernel, turned, [nine_b, fold, pltpu.VMEM((toks, width), F32)]
    )(backs_in, tokp, cotp, slot, gainp, dnormed)
    return mixed.T, token_grad.T


def solution(mesh):
    dp, seq = mesh.devices.shape
    split = Mesh(mesh.devices.reshape(dp, seq // 2, 2), ("dp", "x", "core"))
    every = ("dp", "x", "core")
    flat, deep = P(every, None), P(every, None, None)
    return jax.shard_map(
        shards,
        mesh=split,
        in_specs=(flat, P(), P(), flat, deep, deep, deep, deep, flat),
        out_specs=(flat, flat),
        check_vma=False,
    )
```

```python
import functools

import jax
import jax.numpy as jnp
from jax import lax
from jax.experimental import pallas as pl
from jax.experimental.pallas import tpu as pltpu
from jax.sharding import Mesh, PartitionSpec as P

glu_slope = 1.702
norm_epsilon = 1e-05

LANE = 128
PAIR = 2 * LANE
SLOTS = 8
F32 = jnp.float32
BF16 = jnp.bfloat16


def up_to(n, m):
    return -(-n // m) * m


def mm(a, b):
    return jnp.dot(a, b, preferred_element_type=F32)


def mm_nt(a, b):
    return lax.dot_general(a, b, (((1,), (1,)), ((), ())), preferred_element_type=F32)


def iota(shape, dim):
    return lax.broadcasted_iota(jnp.int32, shape, dim)


def mm_tn(a, b):
    return lax.dot_general(a, b, (((0,), (0,)), ((), ())), preferred_element_type=F32)


def split_matrix(n):
    nat, col = iota((n, n), 0), iota((n, n), 1)
    half = n // 2
    src = jnp.where(col < half, 2 * col, 2 * (col - half) + 1)
    return (nat == src).astype(F32).astype(BF16)


def feature_blocks(width):
    full = width // PAIR * PAIR
    blocks = [(start, PAIR, split_matrix(PAIR)) for start in range(0, full, PAIR)]
    return blocks + ([(full, width - full, split_matrix(width - full))] if width > full else [])


def order_columns(src_ref, dst_ref):
    for start, size, hot in feature_blocks(src_ref.shape[1]):
        dst_ref[:, start : start + size] = mm(src_ref[:, start : start + size], hot).astype(BF16)


def order_rows(src_ref, dst_ref):
    for start, size, hot in feature_blocks(src_ref.shape[0]):
        dst_ref[:, start : start + size] = mm_tn(src_ref[start : start + size, :], hot).astype(BF16)


def restore_rows(load, dst_ref):
    for start, size, hot in feature_blocks(dst_ref.shape[0]):
        dst_ref[start : start + size, :] = mm_nt(hot, load(start, size)).astype(BF16)


def tail_geometry(width):
    tail_at = up_to(width, LANE)
    tail = up_to(-(-tail_at // SLOTS), LANE)
    return tail_at, tail


def slot_hot(slot_t):
    experts, toks = slot_t.shape
    s_idx = iota((experts, SLOTS, toks), 1).astype(F32)
    hot = (slot_t[:, None, :] == s_idx).astype(F32)
    return hot.reshape(experts * SLOTS, toks), (slot_t == float(SLOTS)).astype(F32)


def put_tail(msg_ref, nine, nine_sc, fold_sc, tail_at, tail, width):
    experts = nine.shape[0]
    nine_sc[:, width:] = jnp.zeros((experts, nine_sc.shape[1] - width), F32)
    nine_sc[:, :width] = nine
    fold_lanes(msg_ref, nine_sc, fold_sc, experts, tail_at, tail)


def fold_lanes(msg_ref, nine, fold_sc, experts, tail_at, tail):
    for j in range(tail // LANE):
        for r in range(SLOTS):
            at = r * tail + j * LANE
            fold_sc[j, pl.ds(r, experts, stride=SLOTS), :] = nine[:, at : at + LANE]
        at = tail_at + j * LANE
        msg_ref[:, at : at + LANE] = fold_sc[j].astype(BF16)


def fetch(msg_ref, main_sc, tail_sc, sem, tail_at):
    rows = msg_ref.shape[0]
    pair = (
        pltpu.make_async_copy(
            msg_ref.at[:, pl.ds(0, tail_at)], main_sc.at[pl.ds(0, rows), pl.ds(0, tail_at)], sem.at[0]
        ),
        pltpu.make_async_copy(
            msg_ref.at[:, pl.ds(tail_at, tail_sc.shape[1])], tail_sc, sem.at[1]
        ),
    )
    for copy in pair:
        copy.start()
    for copy in pair:
        copy.wait()


def get_tail(msg_ref, fold_sc, put, tail_at, tail, experts):
    for j in range(tail // LANE):
        at = tail_at + j * LANE
        fold_sc[j] = msg_ref[:, at : at + LANE].astype(F32)
        for r in range(SLOTS):
            put(r * tail + j * LANE, fold_sc[j, pl.ds(r, experts, stride=SLOTS), :].astype(BF16))


def dispatch_rows_kernel(
    tok_ref, gain_ref, router_ref, ids_ref,
    msg_ref, prob_ref, slot_ref, tokp_ref, gainp_ref, routerp_ref,
    normp_sc, gain_sc, nine_sc, fold_sc,
):
    width, toks = tok_ref.shape
    top = ids_ref.shape[0]
    experts = router_ref.shape[0]
    tail_at, tail = tail_geometry(width)
    order_rows(tok_ref, tokp_ref)
    gain_sc[...] = jnp.broadcast_to(gain_ref[...].reshape(1, width), gain_sc.shape)
    order_columns(gain_sc, gainp_ref)
    order_columns(router_ref, routerp_ref)
    tok = tokp_ref[...].astype(F32)
    inv = lax.rsqrt(jnp.sum(tok * tok, axis=1, keepdims=True) / width + norm_epsilon)
    normp_sc[...] = (tok * inv * gainp_ref[0:1, :].astype(F32)).astype(BF16)
    logits = mm_nt(routerp_ref[...], normp_sc[...])
    e_idx = iota((experts, toks), 0)
    chosen = e_idx == ids_ref[0:1, :]
    for k in range(1, top):
        chosen = chosen | (e_idx == ids_ref[k : k + 1, :])
    raised = jnp.where(chosen, jnp.exp(logits), 0.0)
    prob_ref[...] = raised / jnp.sum(raised, axis=0, keepdims=True)
    earlier = (iota((toks, toks), 0) < iota((toks, toks), 1)).astype(F32).astype(BF16)
    rank = mm(chosen.astype(F32).astype(BF16), earlier)
    slot = jnp.where(chosen, rank, -1.0)
    slot_ref[...] = slot
    hot, hot_nine = slot_hot(slot)
    hot = hot.astype(BF16)
    for start in range(0, width, 2 * PAIR):
        stop = min(start + 2 * PAIR, width)
        msg_ref[:, start:stop] = mm(hot, normp_sc[:, start:stop]).astype(BF16)
    msg_ref[:, width:tail_at] = jnp.zeros((msg_ref.shape[0], tail_at - width), BF16)
    nine = mm(hot_nine.astype(BF16), normp_sc[...])
    put_tail(msg_ref, nine, nine_sc, fold_sc, tail_at, tail, width)


def dispatch_grads_kernel(
    cot_ref, prob_ref, slot_ref,
    msg_ref, cotp_ref,
    nine_sc, fold_sc,
):
    width, toks = cot_ref.shape
    experts = prob_ref.shape[0]
    tail_at, tail = tail_geometry(width)
    order_rows(cot_ref, cotp_ref)
    prob = prob_ref[...]
    hot, hot_nine = slot_hot(slot_ref[...])
    spread = jnp.broadcast_to(prob[:, None, :], (experts, SLOTS, toks)).reshape(experts * SLOTS, toks)
    row_prob = jnp.sum(hot * spread, axis=1, keepdims=True)
    nine_prob = jnp.sum(hot_nine * prob, axis=1, keepdims=True)
    hot = hot.astype(BF16)
    for start in range(0, width, 2 * PAIR):
        stop = min(start + 2 * PAIR, width)
        msg_ref[:, start:stop] = (mm(hot, cotp_ref[:, start:stop]) * row_prob).astype(BF16)
    msg_ref[:, width:tail_at] = jnp.zeros((msg_ref.shape[0], tail_at - width), BF16)
    nine = mm(hot_nine.astype(BF16), cotp_ref[...]) * nine_prob
    put_tail(msg_ref, nine, nine_sc, fold_sc, tail_at, tail, width)


def code_value(code):
    m = code & 7
    mag = jnp.maximum(jnp.maximum(m, 2 * m - 4), 4 * m - 16)
    return jnp.where((code & 8) != 0, -mag, mag).astype(F32)


def decode_rows_kernel(rest, words_ref, scales_ref, out_ref, factor_sc):
    groups = scales_ref.shape[0]
    columns = words_ref.shape[1]
    out_ref[:, columns:] = jnp.zeros((out_ref.shape[0], out_ref.shape[1] - columns), BF16)
    per = words_ref.shape[0] // groups
    step = pl.program_id(0)
    last = pl.num_programs(0) - 1
    factor_sc[...] = jnp.exp2((scales_ref[...] - 128).astype(F32))

    def group(g, low_at, high_at):
        for start in range(0, columns, 4 * LANE):
            stop = min(start + 4 * LANE, columns)
            w = words_ref[g * per : (g + 1) * per, start:stop]
            f = factor_sc[g : g + 1, start:stop]
            out_ref[low_at : low_at + per, start:stop] = (code_value(w) * f).astype(BF16)
            out_ref[high_at : high_at + per, start:stop] = (code_value(w >> 4) * f).astype(BF16)

    @pl.when(step < last)
    def _():
        for g in range(groups):
            group(g, g * per, LANE + g * per)

    @pl.when(step == last)
    def _():
        for g in range(rest // per):
            group(g, g * per, rest + g * per)


def decode_cols_kernel(words_ref, scales_ref, out_ref, factor_sc):
    rows, columns = words_ref.shape
    groups = scales_ref.shape[1]
    per = columns // groups
    step_rows = 16
    expand = (iota((groups, columns), 0) == iota((groups, columns), 1) // per).astype(F32).astype(BF16)
    factor_sc[...] = mm(jnp.exp2((scales_ref[...] - 128).astype(F32)).astype(BF16), expand)
    full = columns // LANE * LANE
    rest = columns - full

    def body(i, carry):
        r = pl.ds(pl.multiple_of(i * step_rows, step_rows), step_rows)
        for start in range(0, full, LANE):
            w = words_ref[r, start : start + LANE]
            f = factor_sc[r, start : start + LANE]
            out_ref[r, 2 * start : 2 * start + LANE] = (code_value(w) * f).astype(BF16)
            out_ref[r, 2 * start + LANE : 2 * start + PAIR] = (code_value(w >> 4) * f).astype(BF16)
        if rest:
            w = words_ref[r, full:columns]
            f = factor_sc[r, full:columns]
            both = jnp.concatenate([code_value(w) * f, code_value(w >> 4) * f], axis=1)
            out_ref[r, 2 * full :] = both.astype(BF16)
        return carry

    lax.fori_loop(0, rows // step_rows, body, 0)


def rounded(half_sum):
    return half_sum.astype(BF16).astype(F32)


def ffn_forward_kernel(
    x_ref, gu_own_ref, gu_oth_ref, down_own_ref, down_oth_ref,
    out_ref, coef_own_ref, coef_oth_ref,
    x_sc, pre_sc, act_own_sc, act_oth_sc, res_sc, fold_sc, tail_sc, sem,
    *, width, half, n_up, n_down,
):
    step = pl.program_id(0)
    rows = x_ref.shape[0]
    experts = rows // SLOTS
    all_rows = rows + experts
    tail_at, tail = tail_geometry(width)
    tile_up = gu_own_ref.shape[1]
    tile_down = down_own_ref.shape[1]
    padded = pre_sc.shape[1]

    @pl.when(step == 0)
    def _():
        fetch(x_ref, x_sc, tail_sc, sem, tail_at)

        def put(at, value):
            x_sc[rows:, at : at + LANE] = value

        get_tail(tail_sc, fold_sc, put, 0, tail, experts)

    def up(gu_ref, index):
        at = pl.multiple_of(index * tile_up, tile_up)
        pre_sc[:, pl.ds(at, tile_up)] = mm(x_sc[:, :width], gu_ref[...])

    def finish(act_sc, coef_ref):
        chunk = 16

        def body(i, carry):
            r = pl.ds(pl.multiple_of(i * chunk, chunk), chunk)
            pre = pre_sc[r, :]
            wide = act_sc.shape[1]
            gate = pre[:, :wide]
            lift = pltpu.roll(pre, padded - half, 1)[:, :wide] + 1.0
            sig = jax.nn.sigmoid(glu_slope * gate)
            glu = gate * sig
            act_sc[r, :] = (glu * lift).astype(BF16)
            slope = sig + glu_slope * glu * (1.0 - sig)
            grad_gate = lift * slope
            zero = jnp.zeros((chunk, padded - wide), F32)
            grad_up = pltpu.roll(jnp.concatenate([glu, zero], axis=1), half, 1)
            lanes = iota((chunk, padded), 1)
            coef_ref[r, :] = jnp.where(
                lanes < half, jnp.concatenate([grad_gate, zero], axis=1), grad_up
            )
            return carry

        lax.fori_loop(0, all_rows // chunk, body, 0)

    @pl.when(step < n_up)
    def _():
        up(gu_own_ref, step)

    @pl.when(step == n_up - 1)
    def _():
        finish(act_own_sc, coef_own_ref)

    @pl.when((step >= n_up) & (step < 2 * n_up))
    def _():
        up(gu_oth_ref, step - n_up)

    @pl.when(step == 2 * n_up - 1)
    def _():
        finish(act_oth_sc, coef_oth_ref)

    @pl.when(step >= 2 * n_up)
    def _():
        at = pl.multiple_of((step - 2 * n_up) * tile_down, tile_down)
        res_sc[:, pl.ds(at, tile_down)] = rounded(
            mm(act_own_sc[:, :half], down_own_ref[...])
        ) + rounded(mm(act_oth_sc[:, :half], down_oth_ref[...]))

    @pl.when(step == 2 * n_up + n_down - 1)
    def _():
        emit(out_ref, res_sc, fold_sc, rows, experts, tail_at, tail)


def emit(out_ref, res_sc, fold_sc, rows, experts, tail_at, tail):
    chunk = 32

    def body(i, carry):
        r = pl.ds(pl.multiple_of(i * chunk, chunk), chunk)
        out_ref[r, :tail_at] = res_sc[r, :tail_at].astype(BF16)
        return carry

    lax.fori_loop(0, rows // chunk, body, 0)
    fold_lanes(out_ref, res_sc.at[rows:, :], fold_sc, experts, tail_at, tail)


def ffn_backward_kernel(
    g_ref, coef_own_ref, coef_oth_ref, down_own_ref, down_oth_ref, gu_own_ref, gu_oth_ref,
    out_ref,
    g_sc, back_sc, pre_own_sc, pre_oth_sc, res_sc, fold_sc, tail_sc, sem,
    *, width, half, inner, n_back,
):
    step = pl.program_id(0)
    rows = g_ref.shape[0]
    experts = rows // SLOTS
    all_rows = rows + experts
    tail_at, tail = tail_geometry(width)
    tile = gu_own_ref.shape[0]
    padded = coef_own_ref.shape[1]

    @pl.when(step == 0)
    def _():
        fetch(g_ref, g_sc, tail_sc, sem, tail_at)

        def put(at, value):
            g_sc[rows:, at : at + LANE] = value

        get_tail(tail_sc, fold_sc, put, 0, tail, experts)

    def finish(coef_ref, pre_sc):
        chunk = 16

        def body(i, carry):
            r = pl.ds(pl.multiple_of(i * chunk, chunk), chunk)
            back = back_sc[r, :]
            lanes = iota((chunk, padded), 1)
            twice = jnp.where(lanes < half, back, pltpu.roll(back, half, 1))
            pre_sc[r, :] = (twice * coef_ref[r, :]).astype(BF16)
            return carry

        lax.fori_loop(0, all_rows // chunk, body, 0)

    @pl.when(step == 0)
    def _():
        back_sc[:, :half] = mm_nt(g_sc[:, :width], down_own_ref[...])
        finish(coef_own_ref, pre_own_sc)

    @pl.when(step == 1)
    def _():
        back_sc[:, :half] = mm_nt(g_sc[:, :width], down_oth_ref[...])
        finish(coef_oth_ref, pre_oth_sc)

    @pl.when(step >= 2)
    def _():
        at = pl.multiple_of((step - 2) * tile, tile)
        res_sc[:, pl.ds(at, tile)] = rounded(
            mm_nt(pre_own_sc[:, :inner], gu_own_ref[:, :inner])
        ) + rounded(mm_nt(pre_oth_sc[:, :inner], gu_oth_ref[:, :inner]))

    @pl.when(step == 2 + n_back - 1)
    def _():
        emit(out_ref, res_sc, fold_sc, rows, experts, tail_at, tail)


def combine_out_kernel(
    msg_ref, tokp_ref, cotp_ref, prob_ref, slot_ref, router_ref,
    mixed_ref, dnormed_ref,
    nine_sc, fold_sc, mix_sc,
):
    toks, width = tokp_ref.shape
    experts = prob_ref.shape[0]
    tail_at, tail = tail_geometry(width)

    def put(at, value):
        nine_sc[:, at : at + LANE] = value

    get_tail(msg_ref, fold_sc, put, tail_at, tail, experts)
    prob = prob_ref[...]
    hot, hot_nine = slot_hot(slot_ref[...])
    spread = jnp.broadcast_to(prob[:, None, :], (experts, SLOTS, toks)).reshape(experts * SLOTS, toks)
    weight = jnp.concatenate([hot * spread, hot_nine * prob], axis=0).T
    high = weight.astype(BF16)
    low = (weight - high.astype(F32)).astype(BF16)
    main = experts * SLOTS
    for start in range(0, width, 2 * PAIR):
        stop = min(start + 2 * PAIR, width)
        rows = msg_ref[:, start:stop]
        nine = nine_sc[:, start:stop]
        total = tokp_ref[:, start:stop].astype(F32)
        total = total + mm(high[:, :main], rows) + mm(low[:, :main], rows)
        total = total + mm(high[:, main:], nine) + mm(low[:, main:], nine)
        mix_sc[:, start:stop] = total.astype(BF16)

    restore_rows(lambda start, size: mix_sc[:, start : start + size], mixed_ref)
    cot = cotp_ref[...]
    along = (mm_nt(msg_ref[:, :width], cot) * hot).reshape(experts, SLOTS, toks)
    dprob = jnp.sum(along, axis=1) + mm_nt(nine_sc[:, :width], cot) * hot_nine
    dlogits_t = prob * (dprob - jnp.sum(prob * dprob, axis=0, keepdims=True))
    dlogits = dlogits_t.T
    first = dlogits.astype(BF16)
    left = dlogits - first.astype(F32)
    second = left.astype(BF16)
    third = (left - second.astype(F32)).astype(BF16)
    router = router_ref[...]
    dnormed_ref[...] = mm(first, router) + mm(second, router) + mm(third, router)


def combine_back_kernel(
    msg_ref, tokp_ref, cotp_ref, slot_ref, gain_ref, dnormed_ref,
    grad_ref,
    nine_sc, fold_sc, sum_sc, msg_sc, tok_sc, cot_sc, dn_sc, sem,
):
    toks, width = tokp_ref.shape
    experts = slot_ref.shape[0]
    tail_at, tail = tail_geometry(width)
    step = 4 * PAIR
    pieces = [(at, min(step, tail_at - at)) for at in range(0, tail_at, step)]
    pieces = [(tail_at, tail)] + pieces
    singles = [
        pltpu.make_async_copy(src, dst, sem.at[i])
        for i, (src, dst) in enumerate(((tokp_ref, tok_sc), (dnormed_ref, dn_sc), (cotp_ref, cot_sc)))
    ]
    chunks = [
        pltpu.make_async_copy(
            msg_ref.at[:, pl.ds(at, size)], msg_sc.at[:, pl.ds(at, size)], sem.at[len(singles) + i]
        )
        for i, (at, size) in enumerate(pieces)
    ]
    for copy in singles + chunks:
        copy.start()
    hot, hot_nine = slot_hot(slot_ref[...])
    pick = jnp.concatenate([hot, hot_nine], axis=0).T.astype(BF16)
    main = experts * SLOTS
    for copy in singles:
        copy.wait()
    square = jnp.zeros((toks, 1), F32)
    for start in range(0, width, 2 * PAIR):
        tok = tok_sc[:, start : min(start + 2 * PAIR, width)].astype(F32)
        square = square + jnp.sum(tok * tok, axis=1, keepdims=True)
    inv = lax.rsqrt(square / width + norm_epsilon)
    chunks[0].wait()

    def put(at, value):
        nine_sc[:, at : at + LANE] = value

    get_tail(msg_sc, fold_sc, put, tail_at, tail, experts)
    along = jnp.zeros((toks, 1), F32)
    for copy, (at, size) in zip(chunks[1:], pieces[1:]):
        copy.wait()
        for start in range(at, min(at + size, width), 2 * PAIR):
            stop = min(start + 2 * PAIR, at + size, width)
            total = mm(pick[:, :main], msg_sc[:, start:stop]) + mm(
                pick[:, main:], nine_sc[:, start:stop]
            )
            total = (total + dn_sc[:, start:stop]) * gain_ref[0:1, start:stop].astype(F32)
            sum_sc[:, start:stop] = total
            along = along + jnp.sum(total * tok_sc[:, start:stop].astype(F32), axis=1, keepdims=True)
    cube = inv * inv * inv * (along / width)

    def load(start, size):
        value = (
            cot_sc[:, start : start + size].astype(F32)
            + inv * sum_sc[:, start : start + size]
            - tok_sc[:, start : start + size].astype(F32) * cube
        )
        return value.astype(BF16)

    restore_rows(load, grad_ref)


def params(mib):
    return pltpu.CompilerParams(vmem_limit_bytes=mib * 1024 * 1024)


def once(shape):
    return pl.BlockSpec(shape, lambda *_: (0,) * len(shape), pipeline_mode=pl.Buffered(1))


def simple_call(kernel, outs, scratch):
    return pl.pallas_call(
        kernel, out_shape=outs, scratch_shapes=scratch, compiler_params=params(63)
    )


def struct(shape, dtype):
    return jax.ShapeDtypeStruct(shape, dtype)


def shards(
    tokens, norm_gain, router_weight, expert_ids,
    gate_up_words, gate_up_scales, down_words, down_scales, cotangent,
):
    toks, width = tokens.shape
    experts = router_weight.shape[1]
    word_rows, inner = gate_up_words.shape[1:]
    half, word_cols = down_words.shape[1:]
    tail_at, tail = tail_geometry(width)
    msg_width = tail_at + tail
    rows = experts * SLOTS
    all_rows = rows + experts
    wide = SLOTS * tail
    padded = up_to(inner, PAIR)

    nine_f = pltpu.VMEM((experts, wide), F32)
    nine_b = pltpu.VMEM((experts, wide), BF16)
    fold = pltpu.VMEM((tail // LANE, rows, LANE), F32)
    msg = struct((rows, msg_width), BF16)

    table = struct((experts, toks), F32)
    block = struct((toks, width), BF16)
    row_msg, prob, slot, tokp, gainp, routerp = simple_call(
        dispatch_rows_kernel,
        (msg, table, table, block, struct((16, width), BF16), struct((experts, width), BF16)),
        [pltpu.VMEM((toks, width), BF16), pltpu.VMEM((16, width), BF16), nine_f, fold],
    )(tokens.T, norm_gain, router_weight.T, expert_ids.T)
    row_msg, gate_up_words, down_words = lax.optimization_barrier(
        (row_msg, gate_up_words, down_words)
    )

    def exchange(message):
        shaped = message.reshape(experts, SLOTS, msg_width)
        swapped = lax.all_to_all(shaped, ("dp", "x"), 0, 0, tiled=True)
        return swapped.reshape(rows, msg_width)

    rows_in = exchange(row_msg)
    grad_msg, cotp = simple_call(
        dispatch_grads_kernel, (msg, block), [nine_f, fold]
    )(cotangent.T, prob, slot)
    grads_in = exchange(grad_msg)

    group_rows = word_rows // gate_up_scales.shape[1]
    steps = -(-word_rows // LANE)
    gate_up = pl.pallas_call(
        functools.partial(decode_rows_kernel, word_rows - (steps - 1) * LANE),
        out_shape=struct((2 * word_rows, padded), BF16),
        grid=(steps,),
        in_specs=[
            pl.BlockSpec((LANE, inner), lambda i: (i, 0)),
            pl.BlockSpec((LANE // group_rows, inner), lambda i: (i, 0)),
        ],
        out_specs=pl.BlockSpec((PAIR, padded), lambda i: (i, 0)),
        scratch_shapes=[pltpu.VMEM((LANE // group_rows, inner), F32)],
        compiler_params=params(63),
        name="decode_gate_up",
    )(gate_up_words[0], gate_up_scales[0])
    down_rows = 144
    down = pl.pallas_call(
        decode_cols_kernel,
        out_shape=struct((half, 2 * word_cols), BF16),
        grid=(half // down_rows,),
        in_specs=[
            pl.BlockSpec((down_rows, word_cols), lambda i: (i, 0)),
            pl.BlockSpec((down_rows, down_scales.shape[2]), lambda i: (i, 0)),
        ],
        out_specs=pl.BlockSpec((down_rows, 2 * word_cols), lambda i: (i, 0)),
        scratch_shapes=[pltpu.VMEM((down_rows, word_cols), F32)],
        compiler_params=params(63),
        name="decode_down",
    )(down_words[0], down_scales[0])
    swap = [(0, 1), (1, 0)]
    gate_up_other = lax.ppermute(gate_up, "core", swap)
    down_other = lax.ppermute(down, "core", swap)

    tile = 512
    n_up = -(-inner // tile)
    n_down = -(-width // tile)
    half_wide = up_to(half, LANE)
    coef = struct((all_rows, padded), F32)

    def clip(i, low, count):
        return jnp.clip(i - low, 0, count - 1)

    out_msg, coef_own, coef_oth = pl.pallas_call(
        functools.partial(ffn_forward_kernel, width=width, half=half, n_up=n_up, n_down=n_down),
        out_shape=(msg, coef, coef),
        grid=(2 * n_up + n_down,),
        in_specs=[
            pl.BlockSpec(memory_space=pltpu.HBM),
            pl.BlockSpec((width, tile), lambda i: (0, clip(i, 0, n_up))),
            pl.BlockSpec((width, tile), lambda i: (0, clip(i, n_up, n_up))),
            pl.BlockSpec((half, tile), lambda i: (0, clip(i, 2 * n_up, n_down))),
            pl.BlockSpec((half, tile), lambda i: (0, clip(i, 2 * n_up, n_down))),
        ],
        out_specs=(once((rows, msg_width)), once((all_rows, padded)), once((all_rows, padded))),
        scratch_shapes=[
            pltpu.VMEM((all_rows, wide), BF16),
            pltpu.VMEM((all_rows, padded), F32),
            pltpu.VMEM((all_rows, half_wide), BF16),
            pltpu.VMEM((all_rows, half_wide), BF16),
            pltpu.VMEM((all_rows, n_down * tile), F32),
            fold,
            pltpu.VMEM((rows, tail), BF16),
            pltpu.SemaphoreType.DMA((2,)),
        ],
        compiler_params=params(63),
        name="ffn_forward",
    )(rows_in, gate_up, gate_up_other, down, down_other)
    outs_in = exchange(out_msg)

    back_msg = pl.pallas_call(
        functools.partial(
            ffn_backward_kernel, width=width, half=half, inner=inner, n_back=n_down
        ),
        out_shape=msg,
        grid=(2 + n_down,),
        in_specs=[
            pl.BlockSpec(memory_space=pltpu.HBM),
            once((all_rows, padded)),
            once((all_rows, padded)),
            once((half, width)),
            once((half, width)),
            pl.BlockSpec((tile, padded), lambda i: (clip(i, 2, n_down), 0)),
            pl.BlockSpec((tile, padded), lambda i: (clip(i, 2, n_down), 0)),
        ],
        out_specs=once((rows, msg_width)),
        scratch_shapes=[
            pltpu.VMEM((all_rows, wide), BF16),
            pltpu.VMEM((all_rows, padded), F32),
            pltpu.VMEM((all_rows, padded), BF16),
            pltpu.VMEM((all_rows, padded), BF16),
            pltpu.VMEM((all_rows, n_down * tile), F32),
            fold,
            pltpu.VMEM((rows, tail), BF16),
            pltpu.SemaphoreType.DMA((2,)),
        ],
        compiler_params=params(63),
        name="ffn_backward",
    )(grads_in, coef_own, coef_oth, down, down_other, gate_up, gate_up_other)
    backs_in = exchange(back_msg)

    turned = struct((width, toks), BF16)
    mixed, dnormed = simple_call(
        combine_out_kernel,
        (turned, struct((toks, width), F32)),
        [nine_b, fold, pltpu.VMEM((toks, width), BF16)],
    )(outs_in, tokp, cotp, prob, slot, routerp)
    in_hbm, in_vmem = pl.BlockSpec(memory_space=pltpu.HBM), pl.BlockSpec(memory_space=pltpu.VMEM)
    token_grad = pl.pallas_call(
        combine_back_kernel,
        out_shape=turned,
        in_specs=[in_hbm, in_hbm, in_hbm, in_vmem, in_vmem, in_hbm],
        scratch_shapes=[
            nine_b,
            fold,
            pltpu.VMEM((toks, width), F32),
            pltpu.VMEM((rows, msg_width), BF16),
            pltpu.VMEM((toks, width), BF16),
            pltpu.VMEM((toks, width), BF16),
            pltpu.VMEM((toks, width), F32),
            pltpu.SemaphoreType.DMA((4 + -(-tail_at // (4 * PAIR)),)),
        ],
        compiler_params=params(63),
        name="combine_back",
    )(backs_in, tokp, cotp, slot, gainp, dnormed)
    return mixed.T, token_grad.T


def solution(mesh):
    dp, seq = mesh.devices.shape
    split = Mesh(mesh.devices.reshape(dp, seq // 2, 2), ("dp", "x", "core"))
    every = ("dp", "x", "core")
    flat, deep = P(every, None), P(every, None, None)
    return jax.shard_map(
        shards,
        mesh=split,
        in_specs=(flat, P(), P(), flat, deep, deep, deep, deep, flat),
        out_specs=(flat, flat),
        check_vma=False,
    )
```

```python
import functools

import jax
import jax.numpy as jnp
from jax import lax
from jax.experimental import pallas as pl
from jax.experimental.pallas import tpu as pltpu
from jax.sharding import Mesh, PartitionSpec as P

glu_slope = 1.702
norm_epsilon = 1e-05

LANE = 128
PAIR = 2 * LANE
SLOTS = 8
F32 = jnp.float32
BF16 = jnp.bfloat16


def up_to(n, m):
    return -(-n // m) * m


def mm(a, b):
    return jnp.dot(a, b, preferred_element_type=F32)


def mm_nt(a, b):
    return lax.dot_general(a, b, (((1,), (1,)), ((), ())), preferred_element_type=F32)


def iota(shape, dim):
    return lax.broadcasted_iota(jnp.int32, shape, dim)


def mm_tn(a, b):
    return lax.dot_general(a, b, (((0,), (0,)), ((), ())), preferred_element_type=F32)


def split_matrix(n):
    nat, col = iota((n, n), 0), iota((n, n), 1)
    half = n // 2
    src = jnp.where(col < half, 2 * col, 2 * (col - half) + 1)
    return (nat == src).astype(F32).astype(BF16)


def feature_blocks(width):
    full = width // PAIR * PAIR
    blocks = [(start, PAIR, split_matrix(PAIR)) for start in range(0, full, PAIR)]
    return blocks + ([(full, width - full, split_matrix(width - full))] if width > full else [])


def order_columns(src_ref, dst_ref):
    for start, size, hot in feature_blocks(src_ref.shape[1]):
        dst_ref[:, start : start + size] = mm(src_ref[:, start : start + size], hot).astype(BF16)


def order_rows(src_ref, dst_ref):
    for start, size, hot in feature_blocks(src_ref.shape[0]):
        dst_ref[:, start : start + size] = mm_tn(src_ref[start : start + size, :], hot).astype(BF16)


def restore_rows(load, dst_ref):
    for start, size, hot in feature_blocks(dst_ref.shape[0]):
        dst_ref[start : start + size, :] = mm_nt(hot, load(start, size)).astype(BF16)


def tail_geometry(width):
    tail_at = up_to(width, LANE)
    tail = up_to(-(-tail_at // SLOTS), LANE)
    return tail_at, tail


def slot_hot(slot_t):
    experts, toks = slot_t.shape
    s_idx = iota((experts, SLOTS, toks), 1).astype(F32)
    hot = (slot_t[:, None, :] == s_idx).astype(F32)
    return hot.reshape(experts * SLOTS, toks), (slot_t == float(SLOTS)).astype(F32)


def put_tail(msg_ref, nine, nine_sc, fold_sc, tail_at, tail, width):
    experts = nine.shape[0]
    nine_sc[:, width:] = jnp.zeros((experts, nine_sc.shape[1] - width), F32)
    nine_sc[:, :width] = nine
    fold_lanes(msg_ref, nine_sc, fold_sc, experts, tail_at, tail)


def fold_lanes(msg_ref, nine, fold_sc, experts, tail_at, tail):
    for j in range(tail // LANE):
        for r in range(SLOTS):
            at = r * tail + j * LANE
            fold_sc[j, pl.ds(r, experts, stride=SLOTS), :] = nine[:, at : at + LANE]
        at = tail_at + j * LANE
        msg_ref[:, at : at + LANE] = fold_sc[j].astype(BF16)


def fetch(msg_ref, main_sc, tail_sc, sem, tail_at):
    rows = msg_ref.shape[0]
    pair = (
        pltpu.make_async_copy(
            msg_ref.at[:, pl.ds(0, tail_at)], main_sc.at[pl.ds(0, rows), pl.ds(0, tail_at)], sem.at[0]
        ),
        pltpu.make_async_copy(
            msg_ref.at[:, pl.ds(tail_at, tail_sc.shape[1])], tail_sc, sem.at[1]
        ),
    )
    for copy in pair:
        copy.start()
    for copy in pair:
        copy.wait()


def get_tail(msg_ref, fold_sc, put, tail_at, tail, experts):
    for j in range(tail // LANE):
        at = tail_at + j * LANE
        fold_sc[j] = msg_ref[:, at : at + LANE].astype(F32)
        for r in range(SLOTS):
            put(r * tail + j * LANE, fold_sc[j, pl.ds(r, experts, stride=SLOTS), :].astype(BF16))


def inverse_rms(tok_ref):
    toks, width = tok_ref.shape
    square = jnp.zeros((toks, 1), F32)
    for start in range(0, width, 4 * PAIR):
        tok = tok_ref[:, start : min(start + 4 * PAIR, width)].astype(F32)
        square = square + jnp.sum(tok * tok, axis=1, keepdims=True)
    return lax.rsqrt(square / width + norm_epsilon)


def normalize(tokp_ref, gainp_ref, normp_sc):
    inv = inverse_rms(tokp_ref)
    normp_sc[...] = (tokp_ref[...].astype(F32) * inv * gainp_ref[0:1, :].astype(F32)).astype(BF16)


def dispatch_rows_kernel(
    tok_ref, gain_ref, ids_ref,
    msg_ref, slot_ref, tokp_ref, gainp_ref,
    normp_sc, gain_sc, nine_sc, fold_sc,
):
    width, toks = tok_ref.shape
    top = ids_ref.shape[0]
    experts = slot_ref.shape[0]
    tail_at, tail = tail_geometry(width)
    order_rows(tok_ref, tokp_ref)
    gain_sc[...] = jnp.broadcast_to(gain_ref[...].reshape(1, width), gain_sc.shape)
    order_columns(gain_sc, gainp_ref)
    normalize(tokp_ref, gainp_ref, normp_sc)
    e_idx = iota((experts, toks), 0)
    chosen = e_idx == ids_ref[0:1, :]
    for k in range(1, top):
        chosen = chosen | (e_idx == ids_ref[k : k + 1, :])
    earlier = (iota((toks, toks), 0) < iota((toks, toks), 1)).astype(F32).astype(BF16)
    rank = mm(chosen.astype(F32).astype(BF16), earlier)
    slot = jnp.where(chosen, rank, -1.0)
    slot_ref[...] = slot
    hot, hot_nine = slot_hot(slot)
    hot = hot.astype(BF16)
    for start in range(0, width, 2 * PAIR):
        stop = min(start + 2 * PAIR, width)
        msg_ref[:, start:stop] = mm(hot, normp_sc[:, start:stop]).astype(BF16)
    msg_ref[:, width:tail_at] = jnp.zeros((msg_ref.shape[0], tail_at - width), BF16)
    nine = mm(hot_nine.astype(BF16), normp_sc[...])
    put_tail(msg_ref, nine, nine_sc, fold_sc, tail_at, tail, width)


def dispatch_grads_kernel(
    cot_ref, slot_ref, tokp_ref, gainp_ref, router_ref,
    msg_ref, cotp_ref, prob_ref, routerp_ref,
    normp_sc, nine_sc, fold_sc,
):
    width, toks = cot_ref.shape
    experts = slot_ref.shape[0]
    tail_at, tail = tail_geometry(width)
    order_columns(router_ref, routerp_ref)
    normalize(tokp_ref, gainp_ref, normp_sc)
    logits = mm_nt(routerp_ref[...], normp_sc[...])
    slot = slot_ref[...]
    raised = jnp.where(slot >= 0.0, jnp.exp(logits), 0.0)
    prob = raised / jnp.sum(raised, axis=0, keepdims=True)
    prob_ref[...] = prob
    order_rows(cot_ref, cotp_ref)
    hot, hot_nine = slot_hot(slot)
    spread = jnp.broadcast_to(prob[:, None, :], (experts, SLOTS, toks)).reshape(experts * SLOTS, toks)
    row_prob = jnp.sum(hot * spread, axis=1, keepdims=True)
    nine_prob = jnp.sum(hot_nine * prob, axis=1, keepdims=True)
    hot = hot.astype(BF16)
    for start in range(0, width, 2 * PAIR):
        stop = min(start + 2 * PAIR, width)
        msg_ref[:, start:stop] = (mm(hot, cotp_ref[:, start:stop]) * row_prob).astype(BF16)
    msg_ref[:, width:tail_at] = jnp.zeros((msg_ref.shape[0], tail_at - width), BF16)
    nine = mm(hot_nine.astype(BF16), cotp_ref[...]) * nine_prob
    put_tail(msg_ref, nine, nine_sc, fold_sc, tail_at, tail, width)


def code_value(code):
    m = code & 7
    mag = jnp.maximum(jnp.maximum(m, 2 * m - 4), 4 * m - 16)
    return jnp.where((code & 8) != 0, -mag, mag).astype(F32)


def decode_rows_kernel(rest, words_ref, scales_ref, out_ref, factor_sc):
    groups = scales_ref.shape[0]
    columns = words_ref.shape[1]
    out_ref[:, columns:] = jnp.zeros((out_ref.shape[0], out_ref.shape[1] - columns), BF16)
    per = words_ref.shape[0] // groups
    step = pl.program_id(0)
    last = pl.num_programs(0) - 1
    factor_sc[...] = jnp.exp2((scales_ref[...] - 128).astype(F32))

    def group(g, low_at, high_at):
        for start in range(0, columns, 4 * LANE):
            stop = min(start + 4 * LANE, columns)
            w = words_ref[g * per : (g + 1) * per, start:stop]
            f = factor_sc[g : g + 1, start:stop]
            out_ref[low_at : low_at + per, start:stop] = (code_value(w) * f).astype(BF16)
            out_ref[high_at : high_at + per, start:stop] = (code_value(w >> 4) * f).astype(BF16)

    @pl.when(step < last)
    def _():
        for g in range(groups):
            group(g, g * per, LANE + g * per)

    @pl.when(step == last)
    def _():
        for g in range(rest // per):
            group(g, g * per, rest + g * per)


def decode_cols_kernel(words_ref, scales_ref, out_ref, factor_sc):
    rows, columns = words_ref.shape
    groups = scales_ref.shape[1]
    per = columns // groups
    step_rows = 16
    expand = (iota((groups, columns), 0) == iota((groups, columns), 1) // per).astype(F32).astype(BF16)
    factor_sc[...] = mm(jnp.exp2((scales_ref[...] - 128).astype(F32)).astype(BF16), expand)
    full = columns // LANE * LANE
    rest = columns - full

    def body(i, carry):
        r = pl.ds(pl.multiple_of(i * step_rows, step_rows), step_rows)
        for start in range(0, full, LANE):
            w = words_ref[r, start : start + LANE]
            f = factor_sc[r, start : start + LANE]
            out_ref[r, 2 * start : 2 * start + LANE] = (code_value(w) * f).astype(BF16)
            out_ref[r, 2 * start + LANE : 2 * start + PAIR] = (code_value(w >> 4) * f).astype(BF16)
        if rest:
            w = words_ref[r, full:columns]
            f = factor_sc[r, full:columns]
            both = jnp.concatenate([code_value(w) * f, code_value(w >> 4) * f], axis=1)
            out_ref[r, 2 * full :] = both.astype(BF16)
        return carry

    lax.fori_loop(0, rows // step_rows, body, 0)


def rounded(half_sum):
    return half_sum.astype(BF16).astype(F32)


def ffn_forward_kernel(
    x_ref, gu_own_ref, gu_oth_ref, down_own_ref, down_oth_ref,
    out_ref, coef_own_ref, coef_oth_ref,
    x_sc, pre_sc, act_own_sc, act_oth_sc, res_sc, fold_sc, tail_sc, sem,
    *, width, half, n_up, n_down,
):
    step = pl.program_id(0)
    rows = x_ref.shape[0]
    experts = rows // SLOTS
    all_rows = rows + experts
    tail_at, tail = tail_geometry(width)
    tile_up = gu_own_ref.shape[1]
    tile_down = down_own_ref.shape[1]
    padded = pre_sc.shape[1]

    @pl.when(step == 0)
    def _():
        fetch(x_ref, x_sc, tail_sc, sem, tail_at)

        def put(at, value):
            x_sc[rows:, at : at + LANE] = value

        get_tail(tail_sc, fold_sc, put, 0, tail, experts)

    def up(gu_ref, index):
        at = pl.multiple_of(index * tile_up, tile_up)
        pre_sc[:, pl.ds(at, tile_up)] = mm(x_sc[:, :width], gu_ref[...])

    def finish(act_sc, coef_ref):
        chunk = 16

        def body(i, carry):
            r = pl.ds(pl.multiple_of(i * chunk, chunk), chunk)
            pre = pre_sc[r, :]
            wide = act_sc.shape[1]
            gate = pre[:, :wide]
            lift = pltpu.roll(pre, padded - half, 1)[:, :wide] + 1.0
            sig = jax.nn.sigmoid(glu_slope * gate)
            glu = gate * sig
            act_sc[r, :] = (glu * lift).astype(BF16)
            slope = sig + glu_slope * glu * (1.0 - sig)
            grad_gate = lift * slope
            zero = jnp.zeros((chunk, padded - wide), F32)
            grad_up = pltpu.roll(jnp.concatenate([glu, zero], axis=1), half, 1)
            lanes = iota((chunk, padded), 1)
            coef_ref[r, :] = jnp.where(
                lanes < half, jnp.concatenate([grad_gate, zero], axis=1), grad_up
            )
            return carry

        lax.fori_loop(0, all_rows // chunk, body, 0)

    @pl.when(step < n_up)
    def _():
        up(gu_own_ref, step)

    @pl.when(step == n_up - 1)
    def _():
        finish(act_own_sc, coef_own_ref)

    @pl.when((step >= n_up) & (step < 2 * n_up))
    def _():
        up(gu_oth_ref, step - n_up)

    @pl.when(step == 2 * n_up - 1)
    def _():
        finish(act_oth_sc, coef_oth_ref)

    @pl.when(step >= 2 * n_up)
    def _():
        at = pl.multiple_of((step - 2 * n_up) * tile_down, tile_down)
        res_sc[:, pl.ds(at, tile_down)] = rounded(
            mm(act_own_sc[:, :half], down_own_ref[...])
        ) + rounded(mm(act_oth_sc[:, :half], down_oth_ref[...]))

    @pl.when(step == 2 * n_up + n_down - 1)
    def _():
        emit(out_ref, res_sc, fold_sc, rows, experts, tail_at, tail)


def emit(out_ref, res_sc, fold_sc, rows, experts, tail_at, tail):
    chunk = 32

    def body(i, carry):
        r = pl.ds(pl.multiple_of(i * chunk, chunk), chunk)
        out_ref[r, :tail_at] = res_sc[r, :tail_at].astype(BF16)
        return carry

    lax.fori_loop(0, rows // chunk, body, 0)
    fold_lanes(out_ref, res_sc.at[rows:, :], fold_sc, experts, tail_at, tail)


def ffn_backward_kernel(
    g_ref, coef_own_ref, coef_oth_ref, down_own_ref, down_oth_ref, gu_own_ref, gu_oth_ref,
    out_ref,
    g_sc, back_sc, pre_own_sc, pre_oth_sc, res_sc, fold_sc, tail_sc, sem,
    *, width, half, inner, n_back,
):
    step = pl.program_id(0)
    rows = g_ref.shape[0]
    experts = rows // SLOTS
    all_rows = rows + experts
    tail_at, tail = tail_geometry(width)
    tile = gu_own_ref.shape[0]
    padded = coef_own_ref.shape[1]

    @pl.when(step == 0)
    def _():
        fetch(g_ref, g_sc, tail_sc, sem, tail_at)

        def put(at, value):
            g_sc[rows:, at : at + LANE] = value

        get_tail(tail_sc, fold_sc, put, 0, tail, experts)

    def finish(coef_ref, pre_sc):
        chunk = 16

        def body(i, carry):
            r = pl.ds(pl.multiple_of(i * chunk, chunk), chunk)
            back = back_sc[r, :]
            lanes = iota((chunk, padded), 1)
            twice = jnp.where(lanes < half, back, pltpu.roll(back, half, 1))
            pre_sc[r, :] = (twice * coef_ref[r, :]).astype(BF16)
            return carry

        lax.fori_loop(0, all_rows // chunk, body, 0)

    @pl.when(step == 0)
    def _():
        back_sc[:, :half] = mm_nt(g_sc[:, :width], down_own_ref[...])
        finish(coef_own_ref, pre_own_sc)

    @pl.when(step == 1)
    def _():
        back_sc[:, :half] = mm_nt(g_sc[:, :width], down_oth_ref[...])
        finish(coef_oth_ref, pre_oth_sc)

    @pl.when(step >= 2)
    def _():
        at = pl.multiple_of((step - 2) * tile, tile)
        res_sc[:, pl.ds(at, tile)] = rounded(
            mm_nt(pre_own_sc[:, :inner], gu_own_ref[:, :inner])
        ) + rounded(mm_nt(pre_oth_sc[:, :inner], gu_oth_ref[:, :inner]))

    @pl.when(step == 2 + n_back - 1)
    def _():
        emit(out_ref, res_sc, fold_sc, rows, experts, tail_at, tail)


def combine_out_kernel(
    msg_ref, tokp_ref, cotp_ref, prob_ref, slot_ref, router_ref, gain_ref,
    mixed_ref, base_ref, pick_ref, inv_ref,
    nine_sc, fold_sc, mix_sc,
):
    toks, width = tokp_ref.shape
    experts = prob_ref.shape[0]
    tail_at, tail = tail_geometry(width)

    def put(at, value):
        nine_sc[:, at : at + LANE] = value

    get_tail(msg_ref, fold_sc, put, tail_at, tail, experts)
    prob = prob_ref[...]
    hot, hot_nine = slot_hot(slot_ref[...])
    spread = jnp.broadcast_to(prob[:, None, :], (experts, SLOTS, toks)).reshape(experts * SLOTS, toks)
    weight = jnp.concatenate([hot * spread, hot_nine * prob], axis=0).T
    high = weight.astype(BF16)
    low = (weight - high.astype(F32)).astype(BF16)
    main = experts * SLOTS
    for start in range(0, width, 2 * PAIR):
        stop = min(start + 2 * PAIR, width)
        rows = msg_ref[:, start:stop]
        nine = nine_sc[:, start:stop]
        total = tokp_ref[:, start:stop].astype(F32)
        total = total + mm(high[:, :main], rows) + mm(low[:, :main], rows)
        total = total + mm(high[:, main:], nine) + mm(low[:, main:], nine)
        mix_sc[:, start:stop] = total.astype(BF16)

    restore_rows(lambda start, size: mix_sc[:, start : start + size], mixed_ref)
    cot = cotp_ref[...]
    along = (mm_nt(msg_ref[:, :width], cot) * hot).reshape(experts, SLOTS, toks)
    dprob = jnp.sum(along, axis=1) + mm_nt(nine_sc[:, :width], cot) * hot_nine
    dlogits_t = prob * (dprob - jnp.sum(prob * dprob, axis=0, keepdims=True))
    dlogits = dlogits_t.T
    first = dlogits.astype(BF16)
    left = dlogits - first.astype(F32)
    second = left.astype(BF16)
    third = (left - second.astype(F32)).astype(BF16)
    router = router_ref[...]
    dnormed = mm(first, router) + mm(second, router) + mm(third, router)
    base_ref[...] = dnormed * gain_ref[0:1, :].astype(F32)
    inv = inverse_rms(tokp_ref)
    along = jnp.sum(base_ref[...] * tokp_ref[...].astype(F32), axis=1, keepdims=True)
    cube = inv * inv * inv * (along / width)
    base_ref[...] = (
        cotp_ref[...].astype(F32) + inv * base_ref[...] - tokp_ref[...].astype(F32) * cube
    )
    inv_ref[...] = jnp.broadcast_to(inv, inv_ref.shape)
    pick_ref[...] = jnp.concatenate([hot, hot_nine], axis=0).T.astype(BF16)


def combine_back_kernel(
    msg_ref, tokp_ref, base_ref, pick_ref, inv_ref, gain_ref,
    grad_ref,
    nine_sc, fold_sc, sum_sc, msg_sc, tok_sc, base_sc, sem,
):
    toks, width = tokp_ref.shape
    experts = nine_sc.shape[0]
    main = experts * SLOTS
    tail_at, tail = tail_geometry(width)
    step = 4 * PAIR
    pieces = [(tail_at, tail)] + [(at, min(step, tail_at - at)) for at in range(0, tail_at, step)]
    chunks = [
        pltpu.make_async_copy(
            msg_ref.at[:, pl.ds(at, size)], msg_sc.at[:, pl.ds(at, size)], sem.at[2 + i]
        )
        for i, (at, size) in enumerate(pieces)
    ]
    tok_copy = pltpu.make_async_copy(tokp_ref, tok_sc, sem.at[0])
    base_copy = pltpu.make_async_copy(base_ref, base_sc, sem.at[1])
    copies = [chunks[0], tok_copy] + chunks[1:] + [base_copy]
    for copy in copies:
        copy.start()
    chunks[0].wait()

    def put(at, value):
        nine_sc[:, at : at + LANE] = value

    get_tail(msg_sc, fold_sc, put, tail_at, tail, experts)
    tok_copy.wait()
    along = jnp.zeros((toks, 1), F32)
    for copy, (at, size) in zip(chunks[1:], pieces[1:]):
        copy.wait()
        for start in range(at, min(at + size, width), 2 * PAIR):
            stop = min(start + 2 * PAIR, at + size, width)
            total = mm(pick_ref[:, :main], msg_sc[:, start:stop]) + mm(
                pick_ref[:, main:], nine_sc[:, start:stop]
            )
            total = total * gain_ref[0:1, start:stop].astype(F32)
            sum_sc[:, start:stop] = total
            along = along + jnp.sum(total * tok_sc[:, start:stop].astype(F32), axis=1, keepdims=True)
    base_copy.wait()
    inv = inv_ref[:, 0:1]
    cube = inv * inv * inv * (along / width)

    def load(start, size):
        value = (
            base_sc[:, start : start + size]
            + inv * sum_sc[:, start : start + size]
            - tok_sc[:, start : start + size].astype(F32) * cube
        )
        return value.astype(BF16)

    restore_rows(load, grad_ref)


def params(mib):
    return pltpu.CompilerParams(vmem_limit_bytes=mib * 1024 * 1024)


def once(shape):
    return pl.BlockSpec(shape, lambda *_: (0,) * len(shape), pipeline_mode=pl.Buffered(1))


def simple_call(kernel, outs, scratch):
    return pl.pallas_call(
        kernel, out_shape=outs, scratch_shapes=scratch, compiler_params=params(63)
    )


def struct(shape, dtype):
    return jax.ShapeDtypeStruct(shape, dtype)


def shards(
    tokens, norm_gain, router_weight, expert_ids,
    gate_up_words, gate_up_scales, down_words, down_scales, cotangent,
):
    toks, width = tokens.shape
    experts = router_weight.shape[1]
    word_rows, inner = gate_up_words.shape[1:]
    half, word_cols = down_words.shape[1:]
    tail_at, tail = tail_geometry(width)
    msg_width = tail_at + tail
    rows = experts * SLOTS
    all_rows = rows + experts
    wide = SLOTS * tail
    padded = up_to(inner, PAIR)

    nine_f = pltpu.VMEM((experts, wide), F32)
    nine_b = pltpu.VMEM((experts, wide), BF16)
    fold = pltpu.VMEM((tail // LANE, rows, LANE), F32)
    msg = struct((rows, msg_width), BF16)

    table = struct((experts, toks), F32)
    block = struct((toks, width), BF16)
    row_msg, slot, tokp, gainp = simple_call(
        dispatch_rows_kernel,
        (msg, table, block, struct((16, width), BF16)),
        [pltpu.VMEM((toks, width), BF16), pltpu.VMEM((16, width), BF16), nine_f, fold],
    )(tokens.T, norm_gain, expert_ids.T)
    row_msg, gate_up_words, down_words = lax.optimization_barrier(
        (row_msg, gate_up_words, down_words)
    )

    def exchange(message):
        shaped = message.reshape(experts, SLOTS, msg_width)
        swapped = lax.all_to_all(shaped, ("dp", "x"), 0, 0, tiled=True)
        return swapped.reshape(rows, msg_width)

    rows_in = exchange(row_msg)
    grad_msg, cotp, prob, routerp = simple_call(
        dispatch_grads_kernel,
        (msg, block, table, struct((experts, width), BF16)),
        [pltpu.VMEM((toks, width), BF16), nine_f, fold],
    )(cotangent.T, slot, tokp, gainp, router_weight.T)
    grads_in = exchange(grad_msg)

    group_rows = word_rows // gate_up_scales.shape[1]
    steps = -(-word_rows // LANE)
    gate_up = pl.pallas_call(
        functools.partial(decode_rows_kernel, word_rows - (steps - 1) * LANE),
        out_shape=struct((2 * word_rows, padded), BF16),
        grid=(steps,),
        in_specs=[
            pl.BlockSpec((LANE, inner), lambda i: (i, 0)),
            pl.BlockSpec((LANE // group_rows, inner), lambda i: (i, 0)),
        ],
        out_specs=pl.BlockSpec((PAIR, padded), lambda i: (i, 0)),
        scratch_shapes=[pltpu.VMEM((LANE // group_rows, inner), F32)],
        compiler_params=params(63),
        name="decode_gate_up",
    )(gate_up_words[0], gate_up_scales[0])
    down_rows = 144
    down = pl.pallas_call(
        decode_cols_kernel,
        out_shape=struct((half, 2 * word_cols), BF16),
        grid=(half // down_rows,),
        in_specs=[
            pl.BlockSpec((down_rows, word_cols), lambda i: (i, 0)),
            pl.BlockSpec((down_rows, down_scales.shape[2]), lambda i: (i, 0)),
        ],
        out_specs=pl.BlockSpec((down_rows, 2 * word_cols), lambda i: (i, 0)),
        scratch_shapes=[pltpu.VMEM((down_rows, word_cols), F32)],
        compiler_params=params(63),
        name="decode_down",
    )(down_words[0], down_scales[0])
    swap = [(0, 1), (1, 0)]
    gate_up_other = lax.ppermute(gate_up, "core", swap)
    down_other = lax.ppermute(down, "core", swap)

    tile = 512
    n_up = -(-inner // tile)
    n_down = -(-width // tile)
    half_wide = up_to(half, LANE)
    coef = struct((all_rows, padded), F32)

    def clip(i, low, count):
        return jnp.clip(i - low, 0, count - 1)

    out_msg, coef_own, coef_oth = pl.pallas_call(
        functools.partial(ffn_forward_kernel, width=width, half=half, n_up=n_up, n_down=n_down),
        out_shape=(msg, coef, coef),
        grid=(2 * n_up + n_down,),
        in_specs=[
            pl.BlockSpec(memory_space=pltpu.HBM),
            pl.BlockSpec((width, tile), lambda i: (0, clip(i, 0, n_up))),
            pl.BlockSpec((width, tile), lambda i: (0, clip(i, n_up, n_up))),
            pl.BlockSpec((half, tile), lambda i: (0, clip(i, 2 * n_up, n_down))),
            pl.BlockSpec((half, tile), lambda i: (0, clip(i, 2 * n_up, n_down))),
        ],
        out_specs=(once((rows, msg_width)), once((all_rows, padded)), once((all_rows, padded))),
        scratch_shapes=[
            pltpu.VMEM((all_rows, wide), BF16),
            pltpu.VMEM((all_rows, padded), F32),
            pltpu.VMEM((all_rows, half_wide), BF16),
            pltpu.VMEM((all_rows, half_wide), BF16),
            pltpu.VMEM((all_rows, n_down * tile), F32),
            fold,
            pltpu.VMEM((rows, tail), BF16),
            pltpu.SemaphoreType.DMA((2,)),
        ],
        compiler_params=params(63),
        name="ffn_forward",
    )(rows_in, gate_up, gate_up_other, down, down_other)
    outs_in = exchange(out_msg)

    back_msg = pl.pallas_call(
        functools.partial(
            ffn_backward_kernel, width=width, half=half, inner=inner, n_back=n_down
        ),
        out_shape=msg,
        grid=(2 + n_down,),
        in_specs=[
            pl.BlockSpec(memory_space=pltpu.HBM),
            once((all_rows, padded)),
            once((all_rows, padded)),
            once((half, width)),
            once((half, width)),
            pl.BlockSpec((tile, padded), lambda i: (clip(i, 2, n_down), 0)),
            pl.BlockSpec((tile, padded), lambda i: (clip(i, 2, n_down), 0)),
        ],
        out_specs=once((rows, msg_width)),
        scratch_shapes=[
            pltpu.VMEM((all_rows, wide), BF16),
            pltpu.VMEM((all_rows, padded), F32),
            pltpu.VMEM((all_rows, padded), BF16),
            pltpu.VMEM((all_rows, padded), BF16),
            pltpu.VMEM((all_rows, n_down * tile), F32),
            fold,
            pltpu.VMEM((rows, tail), BF16),
            pltpu.SemaphoreType.DMA((2,)),
        ],
        compiler_params=params(63),
        name="ffn_backward",
    )(grads_in, coef_own, coef_oth, down, down_other, gate_up, gate_up_other)
    backs_in = exchange(back_msg)

    turned = struct((width, toks), BF16)
    mixed, base, pick, inv = simple_call(
        combine_out_kernel,
        (
            turned,
            struct((toks, width), F32),
            struct((toks, all_rows), BF16),
            struct((toks, LANE), F32),
        ),
        [nine_b, fold, pltpu.VMEM((toks, width), BF16)],
    )(outs_in, tokp, cotp, prob, slot, routerp, gainp)
    in_hbm, in_vmem = pl.BlockSpec(memory_space=pltpu.HBM), pl.BlockSpec(memory_space=pltpu.VMEM)
    token_grad = pl.pallas_call(
        combine_back_kernel,
        out_shape=turned,
        in_specs=[in_hbm, in_hbm, in_hbm, in_vmem, in_vmem, in_vmem],
        scratch_shapes=[
            nine_b,
            fold,
            pltpu.VMEM((toks, width), F32),
            pltpu.VMEM((rows, msg_width), BF16),
            pltpu.VMEM((toks, width), BF16),
            pltpu.VMEM((toks, width), F32),
            pltpu.SemaphoreType.DMA((3 + -(-tail_at // (4 * PAIR)),)),
        ],
        compiler_params=params(63),
        name="combine_back",
    )(backs_in, tokp, base, pick, inv, gainp)
    return mixed.T, token_grad.T


def solution(mesh):
    dp, seq = mesh.devices.shape
    split = Mesh(mesh.devices.reshape(dp, seq // 2, 2), ("dp", "x", "core"))
    every = ("dp", "x", "core")
    flat, deep = P(every, None), P(every, None, None)
    return jax.shard_map(
        shards,
        mesh=split,
        in_specs=(flat, P(), P(), flat, deep, deep, deep, deep, flat),
        out_specs=(flat, flat),
        check_vma=False,
    )
```

```python
import functools

import jax
import jax.numpy as jnp
from jax import lax
from jax.experimental import pallas as pl
from jax.experimental.pallas import tpu as pltpu
from jax.sharding import Mesh, PartitionSpec as P

glu_slope = 1.702
norm_epsilon = 1e-05

LANE = 128
PAIR = 2 * LANE
SLOTS = 8
F32 = jnp.float32
BF16 = jnp.bfloat16


def up_to(n, m):
    return -(-n // m) * m


def mm(a, b):
    return jnp.dot(a, b, preferred_element_type=F32)


def mm_nt(a, b):
    return lax.dot_general(a, b, (((1,), (1,)), ((), ())), preferred_element_type=F32)


def iota(shape, dim):
    return lax.broadcasted_iota(jnp.int32, shape, dim)


def mm_tn(a, b):
    return lax.dot_general(a, b, (((0,), (0,)), ((), ())), preferred_element_type=F32)


def split_matrix(n):
    nat, col = iota((n, n), 0), iota((n, n), 1)
    half = n // 2
    src = jnp.where(col < half, 2 * col, 2 * (col - half) + 1)
    return (nat == src).astype(F32).astype(BF16)


def feature_blocks(width):
    full = width // PAIR * PAIR
    blocks = [(start, PAIR, split_matrix(PAIR)) for start in range(0, full, PAIR)]
    return blocks + ([(full, width - full, split_matrix(width - full))] if width > full else [])


def order_columns(src_ref, dst_ref):
    for start, size, hot in feature_blocks(src_ref.shape[1]):
        dst_ref[:, start : start + size] = mm(src_ref[:, start : start + size], hot).astype(BF16)


def order_rows(src_ref, dst_ref):
    for start, size, hot in feature_blocks(src_ref.shape[0]):
        dst_ref[:, start : start + size] = mm_tn(src_ref[start : start + size, :], hot).astype(BF16)


def restore_rows(load, dst_ref):
    for start, size, hot in feature_blocks(dst_ref.shape[0]):
        dst_ref[start : start + size, :] = mm_nt(hot, load(start, size)).astype(BF16)


def tail_geometry(width):
    tail_at = up_to(width, LANE)
    tail = up_to(-(-tail_at // SLOTS), LANE)
    return tail_at, tail


def slot_hot(slot_t):
    experts, toks = slot_t.shape
    s_idx = iota((experts, SLOTS, toks), 1).astype(F32)
    hot = (slot_t[:, None, :] == s_idx).astype(F32)
    return hot.reshape(experts * SLOTS, toks), (slot_t == float(SLOTS)).astype(F32)


def put_tail(msg_ref, nine, nine_sc, fold_sc, tail_at, tail, width):
    experts = nine.shape[0]
    nine_sc[:, width:] = jnp.zeros((experts, nine_sc.shape[1] - width), F32)
    nine_sc[:, :width] = nine
    fold_lanes(msg_ref, nine_sc, fold_sc, experts, tail_at, tail)


def fold_lanes(msg_ref, nine, fold_sc, experts, tail_at, tail):
    for j in range(tail // LANE):
        for r in range(SLOTS):
            at = r * tail + j * LANE
            fold_sc[j, pl.ds(r, experts, stride=SLOTS), :] = nine[:, at : at + LANE]
        at = tail_at + j * LANE
        msg_ref[:, at : at + LANE] = fold_sc[j].astype(BF16)


def fetch(msg_ref, main_sc, tail_sc, sem, tail_at):
    rows = msg_ref.shape[0]
    pair = (
        pltpu.make_async_copy(
            msg_ref.at[:, pl.ds(0, tail_at)], main_sc.at[pl.ds(0, rows), pl.ds(0, tail_at)], sem.at[0]
        ),
        pltpu.make_async_copy(
            msg_ref.at[:, pl.ds(tail_at, tail_sc.shape[1])], tail_sc, sem.at[1]
        ),
    )
    for copy in pair:
        copy.start()
    for copy in pair:
        copy.wait()


def get_tail(msg_ref, fold_sc, put, tail_at, tail, experts):
    for j in range(tail // LANE):
        at = tail_at + j * LANE
        fold_sc[j] = msg_ref[:, at : at + LANE].astype(F32)
        for r in range(SLOTS):
            put(r * tail + j * LANE, fold_sc[j, pl.ds(r, experts, stride=SLOTS), :].astype(BF16))


def inverse_rms(tok_ref):
    toks, width = tok_ref.shape
    square = jnp.zeros((toks, 1), F32)
    for start in range(0, width, 4 * PAIR):
        tok = tok_ref[:, start : min(start + 4 * PAIR, width)].astype(F32)
        square = square + jnp.sum(tok * tok, axis=1, keepdims=True)
    return lax.rsqrt(square / width + norm_epsilon)


def normalize(tokp_ref, gainp_ref, normp_sc):
    inv = inverse_rms(tokp_ref)
    normp_sc[...] = (tokp_ref[...].astype(F32) * inv * gainp_ref[0:1, :].astype(F32)).astype(BF16)


def dispatch_rows_kernel(
    tok_ref, gain_ref, ids_ref,
    msg_ref, slot_ref, tokp_ref, gainp_ref,
    normp_sc, gain_sc, nine_sc, fold_sc, msg_sc, sem,
):
    width, toks = tok_ref.shape
    top = ids_ref.shape[0]
    experts = slot_ref.shape[0]
    tail_at, tail = tail_geometry(width)
    order_rows(tok_ref, tokp_ref)
    gain_sc[...] = jnp.broadcast_to(gain_ref[...].reshape(1, width), gain_sc.shape)
    order_columns(gain_sc, gainp_ref)
    normalize(tokp_ref, gainp_ref, normp_sc)
    e_idx = iota((experts, toks), 0)
    chosen = e_idx == ids_ref[0:1, :]
    for k in range(1, top):
        chosen = chosen | (e_idx == ids_ref[k : k + 1, :])
    earlier = (iota((toks, toks), 0) < iota((toks, toks), 1)).astype(F32).astype(BF16)
    rank = mm(chosen.astype(F32).astype(BF16), earlier)
    slot = jnp.where(chosen, rank, -1.0)
    slot_ref[...] = slot
    hot, hot_nine = slot_hot(slot)
    hot = hot.astype(BF16)
    step = 2 * PAIR
    count = width // step

    def fill(start, stop):
        msg_sc[:, start:stop] = mm(hot, normp_sc[:, start:stop]).astype(BF16)

    def send(index, start, size):
        at = pl.ds(start, size)
        copy = pltpu.make_async_copy(msg_sc.at[:, at], msg_ref.at[:, at], sem.at[index])
        copy.start()
        return copy

    fill(count * step, width)
    msg_sc[:, width:tail_at] = jnp.zeros((msg_sc.shape[0], tail_at - width), BF16)
    nine = mm(hot_nine.astype(BF16), normp_sc[...])
    put_tail(msg_sc, nine, nine_sc, fold_sc, tail_at, tail, width)
    copies = [send(count, count * step, tail_at + tail - count * step)]
    for i in range(count):
        fill(i * step, (i + 1) * step)
        copies.append(send(i, i * step, step))
    for copy in copies:
        copy.wait()


def dispatch_grads_kernel(
    cot_ref, slot_ref, tokp_ref, gainp_ref, router_ref,
    msg_ref, cotp_ref, prob_ref, routerp_ref,
    normp_sc, nine_sc, fold_sc,
):
    width, toks = cot_ref.shape
    experts = slot_ref.shape[0]
    tail_at, tail = tail_geometry(width)
    order_columns(router_ref, routerp_ref)
    normalize(tokp_ref, gainp_ref, normp_sc)
    logits = mm_nt(routerp_ref[...], normp_sc[...])
    slot = slot_ref[...]
    raised = jnp.where(slot >= 0.0, jnp.exp(logits), 0.0)
    prob = raised / jnp.sum(raised, axis=0, keepdims=True)
    prob_ref[...] = prob
    order_rows(cot_ref, cotp_ref)
    hot, hot_nine = slot_hot(slot)
    spread = jnp.broadcast_to(prob[:, None, :], (experts, SLOTS, toks)).reshape(experts * SLOTS, toks)
    row_prob = jnp.sum(hot * spread, axis=1, keepdims=True)
    nine_prob = jnp.sum(hot_nine * prob, axis=1, keepdims=True)
    hot = hot.astype(BF16)
    for start in range(0, width, 2 * PAIR):
        stop = min(start + 2 * PAIR, width)
        msg_ref[:, start:stop] = (mm(hot, cotp_ref[:, start:stop]) * row_prob).astype(BF16)
    msg_ref[:, width:tail_at] = jnp.zeros((msg_ref.shape[0], tail_at - width), BF16)
    nine = mm(hot_nine.astype(BF16), cotp_ref[...]) * nine_prob
    put_tail(msg_ref, nine, nine_sc, fold_sc, tail_at, tail, width)


def code_value(code):
    m = code & 7
    mag = jnp.maximum(jnp.maximum(m, 2 * m - 4), 4 * m - 16)
    return jnp.where((code & 8) != 0, -mag, mag).astype(F32)


def decode_rows_kernel(rest, words_ref, scales_ref, out_ref, factor_sc):
    groups = scales_ref.shape[0]
    columns = words_ref.shape[1]
    out_ref[:, columns:] = jnp.zeros((out_ref.shape[0], out_ref.shape[1] - columns), BF16)
    per = words_ref.shape[0] // groups
    step = pl.program_id(0)
    last = pl.num_programs(0) - 1
    factor_sc[...] = jnp.exp2((scales_ref[...] - 128).astype(F32))

    def group(g, low_at, high_at):
        for start in range(0, columns, 4 * LANE):
            stop = min(start + 4 * LANE, columns)
            w = words_ref[g * per : (g + 1) * per, start:stop]
            f = factor_sc[g : g + 1, start:stop]
            out_ref[low_at : low_at + per, start:stop] = (code_value(w) * f).astype(BF16)
            out_ref[high_at : high_at + per, start:stop] = (code_value(w >> 4) * f).astype(BF16)

    @pl.when(step < last)
    def _():
        for g in range(groups):
            group(g, g * per, LANE + g * per)

    @pl.when(step == last)
    def _():
        for g in range(rest // per):
            group(g, g * per, rest + g * per)


def decode_cols_kernel(words_ref, scales_ref, out_ref, factor_sc):
    rows, columns = words_ref.shape
    groups = scales_ref.shape[1]
    per = columns // groups
    step_rows = 16
    expand = (iota((groups, columns), 0) == iota((groups, columns), 1) // per).astype(F32).astype(BF16)
    factor_sc[...] = mm(jnp.exp2((scales_ref[...] - 128).astype(F32)).astype(BF16), expand)
    full = columns // LANE * LANE
    rest = columns - full

    def body(i, carry):
        r = pl.ds(pl.multiple_of(i * step_rows, step_rows), step_rows)
        for start in range(0, full, LANE):
            w = words_ref[r, start : start + LANE]
            f = factor_sc[r, start : start + LANE]
            out_ref[r, 2 * start : 2 * start + LANE] = (code_value(w) * f).astype(BF16)
            out_ref[r, 2 * start + LANE : 2 * start + PAIR] = (code_value(w >> 4) * f).astype(BF16)
        if rest:
            w = words_ref[r, full:columns]
            f = factor_sc[r, full:columns]
            both = jnp.concatenate([code_value(w) * f, code_value(w >> 4) * f], axis=1)
            out_ref[r, 2 * full :] = both.astype(BF16)
        return carry

    lax.fori_loop(0, rows // step_rows, body, 0)


def rounded(half_sum):
    return half_sum.astype(BF16).astype(F32)


def ffn_forward_kernel(
    x_ref, gu_own_ref, gu_oth_ref, down_own_ref, down_oth_ref,
    out_ref, coef_own_ref, coef_oth_ref,
    x_sc, pre_sc, act_own_sc, act_oth_sc, res_sc, fold_sc, tail_sc, sem,
    *, width, half, n_up, n_down,
):
    step = pl.program_id(0)
    rows = x_ref.shape[0]
    experts = rows // SLOTS
    all_rows = rows + experts
    tail_at, tail = tail_geometry(width)
    tile_up = gu_own_ref.shape[1]
    tile_down = down_own_ref.shape[1]
    padded = pre_sc.shape[1]

    @pl.when(step == 0)
    def _():
        fetch(x_ref, x_sc, tail_sc, sem, tail_at)

        def put(at, value):
            x_sc[rows:, at : at + LANE] = value

        get_tail(tail_sc, fold_sc, put, 0, tail, experts)

    def up(gu_ref, index):
        at = pl.multiple_of(index * tile_up, tile_up)
        pre_sc[:, pl.ds(at, tile_up)] = mm(x_sc[:, :width], gu_ref[...])

    def finish(act_sc, coef_ref):
        chunk = 16

        def body(i, carry):
            r = pl.ds(pl.multiple_of(i * chunk, chunk), chunk)
            pre = pre_sc[r, :]
            wide = act_sc.shape[1]
            gate = pre[:, :wide]
            lift = pltpu.roll(pre, padded - half, 1)[:, :wide] + 1.0
            sig = jax.nn.sigmoid(glu_slope * gate)
            glu = gate * sig
            act_sc[r, :] = (glu * lift).astype(BF16)
            slope = sig + glu_slope * glu * (1.0 - sig)
            grad_gate = lift * slope
            zero = jnp.zeros((chunk, padded - wide), F32)
            grad_up = pltpu.roll(jnp.concatenate([glu, zero], axis=1), half, 1)
            lanes = iota((chunk, padded), 1)
            coef_ref[r, :] = jnp.where(
                lanes < half, jnp.concatenate([grad_gate, zero], axis=1), grad_up
            )
            return carry

        lax.fori_loop(0, all_rows // chunk, body, 0)

    @pl.when(step < n_up)
    def _():
        up(gu_own_ref, step)

    @pl.when(step == n_up - 1)
    def _():
        finish(act_own_sc, coef_own_ref)

    @pl.when((step >= n_up) & (step < 2 * n_up))
    def _():
        up(gu_oth_ref, step - n_up)

    @pl.when(step == 2 * n_up - 1)
    def _():
        finish(act_oth_sc, coef_oth_ref)

    @pl.when(step >= 2 * n_up)
    def _():
        at = pl.multiple_of((step - 2 * n_up) * tile_down, tile_down)
        res_sc[:, pl.ds(at, tile_down)] = rounded(
            mm(act_own_sc[:, :half], down_own_ref[...])
        ) + rounded(mm(act_oth_sc[:, :half], down_oth_ref[...]))

    @pl.when(step == 2 * n_up + n_down - 1)
    def _():
        emit(out_ref, res_sc, fold_sc, rows, experts, tail_at, tail)


def emit(out_ref, res_sc, fold_sc, rows, experts, tail_at, tail):
    chunk = 32

    def body(i, carry):
        r = pl.ds(pl.multiple_of(i * chunk, chunk), chunk)
        out_ref[r, :tail_at] = res_sc[r, :tail_at].astype(BF16)
        return carry

    lax.fori_loop(0, rows // chunk, body, 0)
    fold_lanes(out_ref, res_sc.at[rows:, :], fold_sc, experts, tail_at, tail)


def ffn_backward_kernel(
    g_ref, coef_own_ref, coef_oth_ref, down_own_ref, down_oth_ref, gu_own_ref, gu_oth_ref,
    out_ref,
    g_sc, back_sc, pre_own_sc, pre_oth_sc, res_sc, fold_sc, tail_sc, sem,
    *, width, half, inner, n_back,
):
    step = pl.program_id(0)
    rows = g_ref.shape[0]
    experts = rows // SLOTS
    all_rows = rows + experts
    tail_at, tail = tail_geometry(width)
    tile = gu_own_ref.shape[0]
    padded = coef_own_ref.shape[1]

    @pl.when(step == 0)
    def _():
        fetch(g_ref, g_sc, tail_sc, sem, tail_at)

        def put(at, value):
            g_sc[rows:, at : at + LANE] = value

        get_tail(tail_sc, fold_sc, put, 0, tail, experts)

    def finish(coef_ref, pre_sc):
        chunk = 16

        def body(i, carry):
            r = pl.ds(pl.multiple_of(i * chunk, chunk), chunk)
            back = back_sc[r, :]
            lanes = iota((chunk, padded), 1)
            twice = jnp.where(lanes < half, back, pltpu.roll(back, half, 1))
            pre_sc[r, :] = (twice * coef_ref[r, :]).astype(BF16)
            return carry

        lax.fori_loop(0, all_rows // chunk, body, 0)

    @pl.when(step == 0)
    def _():
        back_sc[:, :half] = mm_nt(g_sc[:, :width], down_own_ref[...])
        finish(coef_own_ref, pre_own_sc)

    @pl.when(step == 1)
    def _():
        back_sc[:, :half] = mm_nt(g_sc[:, :width], down_oth_ref[...])
        finish(coef_oth_ref, pre_oth_sc)

    @pl.when(step >= 2)
    def _():
        at = pl.multiple_of((step - 2) * tile, tile)
        res_sc[:, pl.ds(at, tile)] = rounded(
            mm_nt(pre_own_sc[:, :inner], gu_own_ref[:, :inner])
        ) + rounded(mm_nt(pre_oth_sc[:, :inner], gu_oth_ref[:, :inner]))

    @pl.when(step == 2 + n_back - 1)
    def _():
        emit(out_ref, res_sc, fold_sc, rows, experts, tail_at, tail)


def combine_out_kernel(
    msg_ref, tokp_ref, cotp_ref, prob_ref, slot_ref, router_ref, gain_ref,
    mixed_ref, base_ref, pick_ref, inv_ref,
    nine_sc, fold_sc, mix_sc,
):
    toks, width = tokp_ref.shape
    experts = prob_ref.shape[0]
    tail_at, tail = tail_geometry(width)

    def put(at, value):
        nine_sc[:, at : at + LANE] = value

    get_tail(msg_ref, fold_sc, put, tail_at, tail, experts)
    prob = prob_ref[...]
    hot, hot_nine = slot_hot(slot_ref[...])
    spread = jnp.broadcast_to(prob[:, None, :], (experts, SLOTS, toks)).reshape(experts * SLOTS, toks)
    weight = jnp.concatenate([hot * spread, hot_nine * prob], axis=0).T
    high = weight.astype(BF16)
    low = (weight - high.astype(F32)).astype(BF16)
    main = experts * SLOTS
    for start in range(0, width, 2 * PAIR):
        stop = min(start + 2 * PAIR, width)
        rows = msg_ref[:, start:stop]
        nine = nine_sc[:, start:stop]
        total = tokp_ref[:, start:stop].astype(F32)
        total = total + mm(high[:, :main], rows) + mm(low[:, :main], rows)
        total = total + mm(high[:, main:], nine) + mm(low[:, main:], nine)
        mix_sc[:, start:stop] = total.astype(BF16)

    restore_rows(lambda start, size: mix_sc[:, start : start + size], mixed_ref)
    cot = cotp_ref[...]
    along = (mm_nt(msg_ref[:, :width], cot) * hot).reshape(experts, SLOTS, toks)
    dprob = jnp.sum(along, axis=1) + mm_nt(nine_sc[:, :width], cot) * hot_nine
    dlogits_t = prob * (dprob - jnp.sum(prob * dprob, axis=0, keepdims=True))
    dlogits = dlogits_t.T
    first = dlogits.astype(BF16)
    left = dlogits - first.astype(F32)
    second = left.astype(BF16)
    third = (left - second.astype(F32)).astype(BF16)
    router = router_ref[...]
    dnormed = mm(first, router) + mm(second, router) + mm(third, router)
    base_ref[...] = dnormed * gain_ref[0:1, :].astype(F32)
    inv = inverse_rms(tokp_ref)
    along = jnp.sum(base_ref[...] * tokp_ref[...].astype(F32), axis=1, keepdims=True)
    cube = inv * inv * inv * (along / width)
    base_ref[...] = (
        cotp_ref[...].astype(F32) + inv * base_ref[...] - tokp_ref[...].astype(F32) * cube
    )
    inv_ref[...] = jnp.broadcast_to(inv, inv_ref.shape)
    pick_ref[...] = jnp.concatenate([hot, hot_nine], axis=0).T.astype(BF16)


def combine_back_kernel(
    msg_ref, tokp_ref, base_ref, pick_ref, inv_ref, gain_ref,
    grad_ref,
    nine_sc, fold_sc, sum_sc, msg_sc, tok_sc, base_sc, sem,
):
    toks, width = tokp_ref.shape
    experts = nine_sc.shape[0]
    main = experts * SLOTS
    tail_at, tail = tail_geometry(width)
    step = 4 * PAIR
    pieces = [(tail_at, tail)] + [(at, min(step, tail_at - at)) for at in range(0, tail_at, step)]
    chunks = [
        pltpu.make_async_copy(
            msg_ref.at[:, pl.ds(at, size)], msg_sc.at[:, pl.ds(at, size)], sem.at[2 + i]
        )
        for i, (at, size) in enumerate(pieces)
    ]
    tok_copy = pltpu.make_async_copy(tokp_ref, tok_sc, sem.at[0])
    base_copy = pltpu.make_async_copy(base_ref, base_sc, sem.at[1])
    copies = [chunks[0], tok_copy] + chunks[1:] + [base_copy]
    for copy in copies:
        copy.start()
    chunks[0].wait()

    def put(at, value):
        nine_sc[:, at : at + LANE] = value

    get_tail(msg_sc, fold_sc, put, tail_at, tail, experts)
    tok_copy.wait()
    along = jnp.zeros((toks, 1), F32)
    for copy, (at, size) in zip(chunks[1:], pieces[1:]):
        copy.wait()
        for start in range(at, min(at + size, width), 2 * PAIR):
            stop = min(start + 2 * PAIR, at + size, width)
            total = mm(pick_ref[:, :main], msg_sc[:, start:stop]) + mm(
                pick_ref[:, main:], nine_sc[:, start:stop]
            )
            total = total * gain_ref[0:1, start:stop].astype(F32)
            sum_sc[:, start:stop] = total
            along = along + jnp.sum(total * tok_sc[:, start:stop].astype(F32), axis=1, keepdims=True)
    base_copy.wait()
    inv = inv_ref[:, 0:1]
    cube = inv * inv * inv * (along / width)

    def load(start, size):
        value = (
            base_sc[:, start : start + size]
            + inv * sum_sc[:, start : start + size]
            - tok_sc[:, start : start + size].astype(F32) * cube
        )
        return value.astype(BF16)

    restore_rows(load, grad_ref)


def params(mib):
    return pltpu.CompilerParams(vmem_limit_bytes=mib * 1024 * 1024)


def once(shape):
    return pl.BlockSpec(shape, lambda *_: (0,) * len(shape), pipeline_mode=pl.Buffered(1))


def simple_call(kernel, outs, scratch):
    return pl.pallas_call(
        kernel, out_shape=outs, scratch_shapes=scratch, compiler_params=params(63)
    )


def struct(shape, dtype):
    return jax.ShapeDtypeStruct(shape, dtype)


def shards(
    tokens, norm_gain, router_weight, expert_ids,
    gate_up_words, gate_up_scales, down_words, down_scales, cotangent,
):
    toks, width = tokens.shape
    experts = router_weight.shape[1]
    word_rows, inner = gate_up_words.shape[1:]
    half, word_cols = down_words.shape[1:]
    tail_at, tail = tail_geometry(width)
    msg_width = tail_at + tail
    rows = experts * SLOTS
    all_rows = rows + experts
    wide = SLOTS * tail
    padded = up_to(inner, PAIR)

    nine_f = pltpu.VMEM((experts, wide), F32)
    nine_b = pltpu.VMEM((experts, wide), BF16)
    fold = pltpu.VMEM((tail // LANE, rows, LANE), F32)
    msg = struct((rows, msg_width), BF16)

    table = struct((experts, toks), F32)
    block = struct((toks, width), BF16)
    in_hbm, in_vmem = pl.BlockSpec(memory_space=pltpu.HBM), pl.BlockSpec(memory_space=pltpu.VMEM)
    row_msg, slot, tokp, gainp = pl.pallas_call(
        dispatch_rows_kernel,
        out_shape=(msg, table, block, struct((16, width), BF16)),
        in_specs=[in_vmem] * 3,
        out_specs=(in_hbm, in_vmem, in_vmem, in_vmem),
        scratch_shapes=[
            pltpu.VMEM((toks, width), BF16),
            pltpu.VMEM((16, width), BF16),
            nine_f,
            fold,
            pltpu.VMEM((rows, msg_width), BF16),
            pltpu.SemaphoreType.DMA((1 + width // (2 * PAIR),)),
        ],
        compiler_params=params(63),
        name="dispatch_rows",
    )(tokens.T, norm_gain, expert_ids.T)
    row_msg, gate_up_words, down_words = lax.optimization_barrier(
        (row_msg, gate_up_words, down_words)
    )

    def exchange(message):
        shaped = message.reshape(experts, SLOTS, msg_width)
        swapped = lax.all_to_all(shaped, ("dp", "x"), 0, 0, tiled=True)
        return swapped.reshape(rows, msg_width)

    rows_in = exchange(row_msg)
    grad_msg, cotp, prob, routerp = simple_call(
        dispatch_grads_kernel,
        (msg, block, table, struct((experts, width), BF16)),
        [pltpu.VMEM((toks, width), BF16), nine_f, fold],
    )(cotangent.T, slot, tokp, gainp, router_weight.T)
    grads_in = exchange(grad_msg)

    group_rows = word_rows // gate_up_scales.shape[1]
    steps = -(-word_rows // LANE)
    gate_up = pl.pallas_call(
        functools.partial(decode_rows_kernel, word_rows - (steps - 1) * LANE),
        out_shape=struct((2 * word_rows, padded), BF16),
        grid=(steps,),
        in_specs=[
            pl.BlockSpec((LANE, inner), lambda i: (i, 0)),
            pl.BlockSpec((LANE // group_rows, inner), lambda i: (i, 0)),
        ],
        out_specs=pl.BlockSpec((PAIR, padded), lambda i: (i, 0)),
        scratch_shapes=[pltpu.VMEM((LANE // group_rows, inner), F32)],
        compiler_params=params(63),
        name="decode_gate_up",
    )(gate_up_words[0], gate_up_scales[0])
    down_rows = 144
    down = pl.pallas_call(
        decode_cols_kernel,
        out_shape=struct((half, 2 * word_cols), BF16),
        grid=(half // down_rows,),
        in_specs=[
            pl.BlockSpec((down_rows, word_cols), lambda i: (i, 0)),
            pl.BlockSpec((down_rows, down_scales.shape[2]), lambda i: (i, 0)),
        ],
        out_specs=pl.BlockSpec((down_rows, 2 * word_cols), lambda i: (i, 0)),
        scratch_shapes=[pltpu.VMEM((down_rows, word_cols), F32)],
        compiler_params=params(63),
        name="decode_down",
    )(down_words[0], down_scales[0])
    swap = [(0, 1), (1, 0)]
    gate_up_other = lax.ppermute(gate_up, "core", swap)
    down_other = lax.ppermute(down, "core", swap)

    tile = 512
    n_up = -(-inner // tile)
    n_down = -(-width // tile)
    half_wide = up_to(half, LANE)
    coef = struct((all_rows, padded), F32)

    def clip(i, low, count):
        return jnp.clip(i - low, 0, count - 1)

    out_msg, coef_own, coef_oth = pl.pallas_call(
        functools.partial(ffn_forward_kernel, width=width, half=half, n_up=n_up, n_down=n_down),
        out_shape=(msg, coef, coef),
        grid=(2 * n_up + n_down,),
        in_specs=[
            pl.BlockSpec(memory_space=pltpu.HBM),
            pl.BlockSpec((width, tile), lambda i: (0, clip(i, 0, n_up))),
            pl.BlockSpec((width, tile), lambda i: (0, clip(i, n_up, n_up))),
            pl.BlockSpec((half, tile), lambda i: (0, clip(i, 2 * n_up, n_down))),
            pl.BlockSpec((half, tile), lambda i: (0, clip(i, 2 * n_up, n_down))),
        ],
        out_specs=(once((rows, msg_width)), once((all_rows, padded)), once((all_rows, padded))),
        scratch_shapes=[
            pltpu.VMEM((all_rows, wide), BF16),
            pltpu.VMEM((all_rows, padded), F32),
            pltpu.VMEM((all_rows, half_wide), BF16),
            pltpu.VMEM((all_rows, half_wide), BF16),
            pltpu.VMEM((all_rows, n_down * tile), F32),
            fold,
            pltpu.VMEM((rows, tail), BF16),
            pltpu.SemaphoreType.DMA((2,)),
        ],
        compiler_params=params(63),
        name="ffn_forward",
    )(rows_in, gate_up, gate_up_other, down, down_other)
    outs_in = exchange(out_msg)

    back_msg = pl.pallas_call(
        functools.partial(
            ffn_backward_kernel, width=width, half=half, inner=inner, n_back=n_down
        ),
        out_shape=msg,
        grid=(2 + n_down,),
        in_specs=[
            pl.BlockSpec(memory_space=pltpu.HBM),
            once((all_rows, padded)),
            once((all_rows, padded)),
            once((half, width)),
            once((half, width)),
            pl.BlockSpec((tile, padded), lambda i: (clip(i, 2, n_down), 0)),
            pl.BlockSpec((tile, padded), lambda i: (clip(i, 2, n_down), 0)),
        ],
        out_specs=once((rows, msg_width)),
        scratch_shapes=[
            pltpu.VMEM((all_rows, wide), BF16),
            pltpu.VMEM((all_rows, padded), F32),
            pltpu.VMEM((all_rows, padded), BF16),
            pltpu.VMEM((all_rows, padded), BF16),
            pltpu.VMEM((all_rows, n_down * tile), F32),
            fold,
            pltpu.VMEM((rows, tail), BF16),
            pltpu.SemaphoreType.DMA((2,)),
        ],
        compiler_params=params(63),
        name="ffn_backward",
    )(grads_in, coef_own, coef_oth, down, down_other, gate_up, gate_up_other)
    backs_in = exchange(back_msg)

    turned = struct((width, toks), BF16)
    mixed, base, pick, inv = simple_call(
        combine_out_kernel,
        (
            turned,
            struct((toks, width), F32),
            struct((toks, all_rows), BF16),
            struct((toks, LANE), F32),
        ),
        [nine_b, fold, pltpu.VMEM((toks, width), BF16)],
    )(outs_in, tokp, cotp, prob, slot, routerp, gainp)
    in_hbm, in_vmem = pl.BlockSpec(memory_space=pltpu.HBM), pl.BlockSpec(memory_space=pltpu.VMEM)
    token_grad = pl.pallas_call(
        combine_back_kernel,
        out_shape=turned,
        in_specs=[in_hbm, in_hbm, in_hbm, in_vmem, in_vmem, in_vmem],
        scratch_shapes=[
            nine_b,
            fold,
            pltpu.VMEM((toks, width), F32),
            pltpu.VMEM((rows, msg_width), BF16),
            pltpu.VMEM((toks, width), BF16),
            pltpu.VMEM((toks, width), F32),
            pltpu.SemaphoreType.DMA((3 + -(-tail_at // (4 * PAIR)),)),
        ],
        compiler_params=params(63),
        name="combine_back",
    )(backs_in, tokp, base, pick, inv, gainp)
    return mixed.T, token_grad.T


def solution(mesh):
    dp, seq = mesh.devices.shape
    split = Mesh(mesh.devices.reshape(dp, seq // 2, 2), ("dp", "x", "core"))
    every = ("dp", "x", "core")
    flat, deep = P(every, None), P(every, None, None)
    return jax.shard_map(
        shards,
        mesh=split,
        in_specs=(flat, P(), P(), flat, deep, deep, deep, deep, flat),
        out_specs=(flat, flat),
        check_vma=False,
    )
```
